128 devices in a mesh: view: 4 (over y), tile: 32 (over z, x, core).
Axes of the slice: x: 4, y: 4, z: 4, core: 2. Of those that a mesh axis runs over, the one named last changes fastest.
Arguments:
- estimate: float32 [128, 768, 512], P(None, 'tile'), may hold values from 0.5 to 2
- view_stacks: float32 [4, 128, 768, 512], P('view', 'tile'), may hold values from 0 to 4
- profile_z: float32 [4, 31], P('view'), may hold values from 0.2 to 1
- profile_y: float32 [4, 15], P('view'), may hold values from 0.2 to 1
- profile_x: float32 [4, 15], P('view'), may hold values from 0.2 to 1
- offsets: int32 [4], P('view'), may hold values from -16 to 16, as said below
- coverage: int32 [32, 4], P('tile'), may hold values from 0 to 1, as said below
Outputs:
- new_estimate: float32 [128, 768, 512], P(None, 'tile')
The draws below stay inside these ranges and needn't reach their ends.
Inputs may be any that keep to these rules, and one draw needn't show every extreme that they name: `offsets`: some view has offset 16 and some view has offset -16. `coverage`: every tile is intersected by at least one view.
All inputs are finite; a program needn't handle non-finite values.
Results may differ from the reference program's by a relative error of at most 0.0001.
Values sent between devices are 32-bit elements; how exact they have to be, the bound alone decides.
A program may use at most 192 MiB of HBM per device.

```python
import math
import jax
import jax.numpy as jnp
from jax import lax

Z = 128
YD = 24
X = 512
KZ = 31
KY = 15
KX = 15
MAXOFF = 16
VIEWS = 4
TILES = 32
Y = 768


def draw_offsets(key, part):
    base = jax.random.randint(key, (VIEWS,), -MAXOFF, MAXOFF + 1)
    order = jax.random.permutation(jax.random.fold_in(key, 7), VIEWS)
    base = base.at[order[0]].set(MAXOFF)
    base = base.at[order[1]].set(-MAXOFF)
    return base.astype(jnp.int32)


def draw_coverage(key, part):
    first = jax.random.fold_in(key, 11)
    second = jax.random.fold_in(key, 13)
    levels = jax.random.randint(first, (TILES, VIEWS), 0, 5)
    bits = (levels < 3).astype(jnp.int32)
    chosen = jax.random.randint(second, (TILES,), 0, VIEWS)
    columns = jnp.arange(VIEWS, dtype=jnp.int32)
    onehot = (columns[None, :] == chosen[:, None]).astype(jnp.int32)
    return jnp.maximum(bits, onehot).astype(jnp.int32)


def block_scale(stream_key, shape, shards, smallest, largest):
    level, own = 1.0, jax.random.fold_in(stream_key, 6)
    for axis_at, blocks in shards:
        draws = jnp.exp(jax.random.uniform(jax.random.fold_in(own, axis_at), (blocks,), jnp.float32, smallest / len(shards), largest / len(shards)))
        level = level * jnp.repeat(draws, shape[axis_at] // blocks).reshape([-1 if axis == axis_at else 1 for axis in range(len(shape))])
    return level


def setup_inputs(seed: int = 0) -> dict:
    seeds = jax.random.split(jax.random.key(seed), 8)
    estimate = jnp.clip(0.5 + 1.5 * jax.random.uniform(seeds[0], (Z, Y, X), jnp.float32) ** block_scale(seeds[0], (Z, Y, X), ((1, 32),), -0.2, 0.2), 0.5, 2.0)
    view_stacks = jnp.clip(4.0 * jax.random.uniform(seeds[1], (VIEWS, Z, Y, X), jnp.float32) ** block_scale(seeds[1], (VIEWS, Z, Y, X), ((0, 4), (1, 32)), -0.2, 0.2), 0.0, 4.0)
    profile_z = jnp.clip(jnp.exp(math.log(1.0) - 1.609438 * jax.random.uniform(seeds[2], (VIEWS, KZ), jnp.float32) ** block_scale(seeds[2], (VIEWS, KZ), ((0, 4),), -0.2, 0.2)), 0.2, 1.0)
    profile_y = jnp.clip(jnp.exp(math.log(1.0) - 1.609438 * jax.random.uniform(seeds[3], (VIEWS, KY), jnp.float32) ** block_scale(seeds[3], (VIEWS, KY), ((0, 4),), -0.2, 0.2)), 0.2, 1.0)
    profile_x = jnp.clip(jnp.exp(math.log(1.0) - 1.609438 * jax.random.uniform(seeds[4], (VIEWS, KX), jnp.float32) ** block_scale(seeds[4], (VIEWS, KX), ((0, 4),), -0.2, 0.2)), 0.2, 1.0)
    offsets = draw_offsets(jax.random.fold_in(seeds[7], 71), 0)
    coverage = draw_coverage(jax.random.fold_in(seeds[7], 71), 0)
    return {"estimate": estimate, "view_stacks": view_stacks, "profile_z": profile_z, "profile_y": profile_y, "profile_x": profile_x, "offsets": offsets, "coverage": coverage}


def correlate(field, kernel, along):
    taps_count = kernel.shape[0]
    half = (taps_count - 1) // 2
    widths = [(0, 0), (0, 0), (0, 0)]
    widths[along] = (half, half)
    padded = jnp.pad(field, widths)
    extent = field.shape[along]
    summed = jnp.zeros(field.shape, jnp.float32)
    for tap_index in range(taps_count):
        summed = summed + kernel[tap_index] * lax.slice_in_dim(padded, tap_index, tap_index + extent, axis=along)
    return summed


def blur_three(field, weights_z, weights_y, weights_x):
    result = correlate(field, weights_z, 0)
    result = correlate(result, weights_y, 1)
    return correlate(result, weights_x, 2)


def reference(estimate, view_stacks, profile_z, profile_y, profile_x, offsets, coverage):
    view_count = jnp.sum(coverage, axis=1).astype(jnp.float32)
    merged = jnp.zeros(estimate.shape, jnp.float32)
    for view_id in range(VIEWS):
        weights_z = profile_z[view_id] / jnp.sum(profile_z[view_id])
        weights_y = profile_y[view_id] / jnp.sum(profile_y[view_id])
        weights_x = profile_x[view_id] / jnp.sum(profile_x[view_id])
        padded = jnp.pad(view_stacks[view_id], ((0, 0), (0, 0), (MAXOFF, MAXOFF)))
        start = (MAXOFF + offsets[view_id]).astype(jnp.int32)
        registered = lax.dynamic_slice_in_dim(padded, start, X, 2)
        blurred = blur_three(estimate, weights_z, weights_y, weights_x)
        quotient = registered / blurred
        back_blur = blur_three(quotient, weights_z[::-1], weights_y[::-1], weights_x[::-1])
        tile_weight = jnp.repeat(coverage[:, view_id].astype(jnp.float32), YD)
        merged = merged + tile_weight[None, :, None] * back_blur
    tile_count = jnp.repeat(view_count, YD)
    return estimate * merged / tile_count[None, :, None]
```

```python
import functools

import jax
import jax.numpy as jnp
from jax import lax
from jax.experimental import pallas as pl
from jax.experimental.pallas import tpu as pltpu
from jax.sharding import PartitionSpec as P

MESH = pl.DeviceIdType.MESH
CORES = 2
LANES = 128
F32 = jnp.float32
BF16 = jnp.bfloat16


def rl_kernel(
    dims,
    est_hbm,
    stack_hbm,
    pz_ref,
    py_ref,
    px_ref,
    off_ref,
    cov_ref,
    out_hbm,
    slab,
    reg,
    est_ext,
    zb,
    q_ext,
    part,
    r1,
    r2,
    out_buf,
    yq,
    az,
    azt,
    wx,
    wxt,
    slab_sem,
    est_load,
    own_sem,
    est_send,
    est_recv,
    a2a_send,
    a2a_recv,
    qh_send,
    qh_recv,
    s1_send,
    s1_recv,
    s2_send,
    s2_recv,
    g1_send,
    g1_recv,
    g2_send,
    g2_recv,
    out_sem,
):
    nv, nt, tx, nz, ny, nx, kz, ky, kx = dims
    planes = nz // nt
    chunks = nx // LANES
    half_y = ky // 2
    half_z = kz // 2
    half_x = kx // 2
    pad = 8
    tz = nt // (tx * CORES)
    blk = nz // nv
    hb = blk // 2

    me_v = lax.axis_index("view")
    me_t = lax.axis_index("tile")
    up = lax.rem(me_v + 1, nv)
    down = lax.rem(me_v + nv - 1, nv)
    across = lax.rem(me_v + 2, nv)
    core = lax.rem(me_t, CORES)
    at_x = lax.rem(me_t // CORES, tx)
    at_z = me_t // (CORES * tx)

    def at(v, t):
        return {"view": v, "tile": t}

    def peer(k):
        c = lax.rem(core + k, CORES)
        x = lax.rem(at_x + k // CORES, tx)
        z = lax.rem(at_z + k // (CORES * tx), tz)
        return (z * tx + x) * CORES + c

    def order(i):
        return lax.rem(i * 11, nt)

    def lanes(c):
        return pl.ds(c * LANES, LANES)

    def load_est(c):
        return pltpu.make_async_copy(
            est_hbm.at[:, :, lanes(c)], est_ext.at[c, :, pl.ds(pad, ny), :], est_load.at[c]
        )

    load_slab = pltpu.make_async_copy(stack_hbm.at[0], slab, slab_sem)
    load_slab.start()
    for c in range(chunks):
        load_est(c).start()

    barrier = pltpu.get_barrier_semaphore()

    def greet(k, carry):
        pl.semaphore_signal(barrier, inc=1, device_id=at(me_v, peer(k)), device_id_type=MESH)
        return carry

    lax.fori_loop(1, nt, greet, 0)
    for v in (up, down):
        pl.semaphore_signal(barrier, inc=1, device_id=at(v, me_t), device_id_type=MESH)
    pl.semaphore_wait(barrier, nt - 1 + 2)

    def est_copy(c, side):
        target = me_t - 1 if side == 0 else me_t + 1
        rows = pl.ds(0, pad) if side == 0 else pl.ds(ny - pad, pad)
        into = pl.ds(pad + ny, pad) if side == 0 else pl.ds(0, pad)
        return pltpu.make_async_remote_copy(
            src_ref=est_hbm.at[:, rows, lanes(c)],
            dst_ref=est_ext.at[c, :, into, :],
            send_sem=est_send.at[c, side],
            recv_sem=est_recv.at[c, side],
            device_id=at(me_v, lax.rem(target + nt, nt)),
            device_id_type=MESH,
        )

    has_left = me_t > 0
    has_right = me_t < nt - 1

    @pl.when(has_left)
    def _():
        for c in range(chunks):
            est_copy(c, 0).start()

    @pl.when(has_right)
    def _():
        for c in range(chunks):
            est_copy(c, 1).start()

    off = off_ref[0]
    turn = lax.rem(nx - off, nx)
    load_slab.wait()
    rows_block = 64
    lane = lax.broadcasted_iota(jnp.int32, (rows_block, nx), 1) + off
    inside = (lane >= 0) & (lane < nx)
    per_plane = slab.shape[1] // rows_block

    def shift(i, carry):
        p = i // per_plane
        r = pl.ds(pl.multiple_of(lax.rem(i, per_plane) * rows_block, rows_block), rows_block)
        slab[p, r, :] = jnp.where(inside, pltpu.roll(slab[p, r, :], turn, 1), 0.0)
        return carry

    lax.fori_loop(0, planes * per_plane, shift, 0)

    my_planes = pl.ds(me_t * planes, planes)

    def a2a_copy(c, t):
        return pltpu.make_async_remote_copy(
            src_ref=slab.at[:, pl.ds(pl.multiple_of(t * ny, 8), ny), lanes(c)],
            dst_ref=reg.at[c, my_planes],
            send_sem=a2a_send.at[c],
            recv_sem=a2a_recv.at[c],
            device_id=at(me_v, t),
            device_id_type=MESH,
        )

    for c in range(chunks):

        def send(i, carry, c=c):
            a2a_copy(c, peer(order(i))).start()
            return carry

        lax.fori_loop(1, nt, send, 0)

    def own_planes(c):
        mine = slab.at[:, pl.ds(pl.multiple_of(me_t * ny, 8), ny), lanes(c)]
        return pltpu.make_async_copy(mine, reg.at[c, my_planes], own_sem.at[c])

    for c in range(chunks):
        own_planes(c).start()

    def total(ref, count):
        return lax.fori_loop(1, count, lambda a, s: s + ref[0, a], ref[0, 0])

    def bands(ref, count, gap, scale):
        zero = jnp.zeros(gap.shape, F32)
        full = lax.fori_loop(0, count, lambda a, m: m + jnp.where(gap == a, ref[0, a], 0.0), zero)
        full = full / scale
        hi = full.astype(BF16)
        lo = (full - hi.astype(F32)).astype(BF16)
        return hi, lo

    scale_zy = jnp.full((nz, nz), total(pz_ref, kz), F32) * jnp.full((nz, nz), total(py_ref, ky), F32)
    row = lax.broadcasted_iota(jnp.int32, (nz, nz), 0)
    col = lax.broadcasted_iota(jnp.int32, (nz, nz), 1)
    for ref, gap in ((az, col - row + half_z), (azt, row - col + half_z)):
        hi, lo = bands(pz_ref, kz, gap, scale_zy)
        ref[...] = jnp.concatenate(
            [jnp.concatenate([hi, hi], axis=1), jnp.concatenate([lo, lo], axis=1)], axis=0
        )
    wide = (3 * LANES, LANES)
    scale_x = jnp.full(wide, total(px_ref, kx), F32)
    row = lax.broadcasted_iota(jnp.int32, wide, 0)
    col = lax.broadcasted_iota(jnp.int32, wide, 1) + LANES
    for ref, gap in ((wx, row - col + half_x), (wxt, col - row + half_x)):
        hi, lo = bands(px_ref, kx, gap, scale_x)
        ref[...] = jnp.concatenate([hi, lo], axis=1)

    def split(v):
        hi = v.astype(BF16)
        return hi, (v - hi.astype(F32)).astype(BF16)

    def z_pass(matrix, v):
        hi, lo = split(v)
        r = jnp.dot(matrix[...], jnp.concatenate([hi, lo], axis=0), preferred_element_type=F32)
        return r[:nz] + r[nz:]

    def x_pass(matrix, src, y0, count, c):
        first, last = max(c - 1, 0), min(c + 1, chunks - 1)
        v = src[pl.ds(y0, count), :, first * LANES : (last + 1) * LANES]
        v = v.reshape(count * nz, v.shape[2])
        hi, lo = split(v)
        w = matrix[(first - c + 1) * LANES : (last - c + 2) * LANES, :]
        r = jnp.dot(
            jnp.concatenate([hi, lo], axis=1),
            jnp.concatenate([w, w], axis=0),
            preferred_element_type=F32,
        )
        return r[:, :LANES] + r[:, LANES:]

    for c in range(chunks):
        load_est(c).wait()

    @pl.when(has_left)
    def _():
        for c in range(chunks):
            est_copy(c, 1).wait_recv()

    @pl.when(has_right)
    def _():
        for c in range(chunks):
            est_copy(c, 0).wait_recv()

    rows_ext = ny + 2 * pad

    def clear_edge(start):
        def body(i, carry):
            for c in range(chunks):
                est_ext[c, i, pl.ds(start, pad), :] = jnp.zeros((pad, LANES), F32)
            return carry

        lax.fori_loop(0, nz, body, 0)

    @pl.when(jnp.logical_not(has_left))
    def _():
        clear_edge(0)

    @pl.when(jnp.logical_not(has_right))
    def _():
        clear_edge(pad + ny)

    est_rows = est_ext.reshape(chunks, nz * rows_ext, LANES)
    first_row = pad - half_y

    def blur_z(i, carry):
        rows = pl.ds(i + first_row, nz, stride=rows_ext)
        zb[i] = z_pass(az, jnp.concatenate([est_rows[c, rows, :] for c in range(chunks)], axis=1))
        return carry

    lax.fori_loop(0, ny + 2 * half_y, blur_z, 0)

    zblock = min(32, nz)

    def blur_y(y, carry):
        def inner(j, carry):
            zs = pl.ds(pl.multiple_of(j * zblock, zblock), zblock)
            acc = py_ref[0, 0] * zb[y, zs, :]
            for b in range(1, ky):
                acc = acc + py_ref[0, b] * zb[y + b, zs, :]
            part[y, zs, :] = acc
            return carry

        return lax.fori_loop(0, nz // zblock, inner, carry)

    lax.fori_loop(0, ny, blur_y, 0)

    ygroup = 4

    def blur_x(i, carry):
        y0 = i * ygroup
        for c in range(chunks):
            r = x_pass(wx, part, y0, ygroup, c)
            q_ext[pl.ds(half_y + y0, ygroup), :, lanes(c)] = r.reshape(ygroup, nz, LANES)
        return carry

    lax.fori_loop(0, ny // ygroup, blur_x, 0)

    halo = jnp.zeros((half_y, nz, nx), F32)

    @pl.when(jnp.logical_not(has_left))
    def _():
        q_ext[pl.ds(0, half_y)] = halo

    @pl.when(jnp.logical_not(has_right))
    def _():
        q_ext[pl.ds(half_y + ny, half_y)] = halo

    cov = jnp.full((nz, LANES), cov_ref[0, me_v].astype(F32), F32)
    count = cov_ref[0, 0]
    for v in range(1, nv):
        count = count + cov_ref[0, v]
    count = jnp.full((ny, LANES), count.astype(F32), F32)

    for c in range(chunks):
        own_planes(c).wait()
    reg_rows = reg.reshape(chunks, nz * ny, LANES)

    def qh_copy(c, side):
        target = me_t - 1 if side == 0 else me_t + 1
        rows = pl.ds(half_y, half_y) if side == 0 else pl.ds(ny, half_y)
        into = pl.ds(half_y + ny, half_y) if side == 0 else pl.ds(0, half_y)
        return pltpu.make_async_remote_copy(
            src_ref=q_ext.at[rows, :, lanes(c)],
            dst_ref=q_ext.at[into, :, lanes(c)],
            send_sem=qh_send.at[c, side],
            recv_sem=qh_recv.at[c, side],
            device_id=at(me_v, lax.rem(target + nt, nt)),
            device_id_type=MESH,
        )

    def quotient(c):
        arrived = reg.at[c, pl.ds(0, nz - planes)]
        pltpu.make_async_copy(arrived, arrived, a2a_recv.at[c]).wait()

        def body(y, carry):
            v = reg_rows[c, pl.ds(y, nz, stride=ny), :]
            q_ext[half_y + y, :, lanes(c)] = v / q_ext[half_y + y, :, lanes(c)]
            return carry

        lax.fori_loop(0, ny, body, 0)

        @pl.when(has_left)
        def _():
            qh_copy(c, 0).start()

        @pl.when(has_right)
        def _():
            qh_copy(c, 1).start()

    def back_yz(c):
        @pl.when(has_left)
        def _():
            qh_copy(c, 1).wait_recv()

        @pl.when(has_right)
        def _():
            qh_copy(c, 0).wait_recv()

        def body(i, carry):
            for k in range(2):
                acc = py_ref[0, ky - 1] * q_ext[2 * i + k, :, lanes(c)]
                for b in range(1, ky):
                    acc = acc + py_ref[0, ky - 1 - b] * q_ext[2 * i + k + b, :, lanes(c)]
                yq[:, k * LANES : (k + 1) * LANES] = acc
            r = z_pass(azt, yq[...])
            for k in range(2):
                zb[2 * i + k, :, lanes(c)] = r[:, k * LANES : (k + 1) * LANES]
            return carry

        lax.fori_loop(0, ny // 2, body, 0)

    sums = reg

    def back_x(c):
        def body(i, carry):
            r = x_pass(wxt, zb, i * ygroup, ygroup, c).reshape(ygroup, nz, LANES)
            for k in range(ygroup):
                reg_rows[c, pl.ds(i * ygroup + k, nz, stride=ny), :] = cov * r[k]
            return carry

        lax.fori_loop(0, ny // ygroup, body, 0)

    def copy_to(src, dst, send, recv, c, d):
        return pltpu.make_async_remote_copy(
            src_ref=src,
            dst_ref=dst,
            send_sem=send.at[c, d],
            recv_sem=recv.at[c, d],
            device_id=at(up if d == 0 else down, me_t),
            device_id_type=MESH,
        )

    def s1_copy(c, d):
        start = across * blk + (0 if d == 0 else hb)
        return copy_to(sums.at[c, pl.ds(start, hb)], r1.at[d, c], s1_send, s1_recv, c, d)

    def s2_copy(c, d):
        start = (up if d == 0 else down) * blk
        return copy_to(sums.at[c, pl.ds(start, blk)], r2.at[d, c], s2_send, s2_recv, c, d)

    def g1_copy(c, d):
        mine = out_buf.at[c, pl.ds(me_v * blk, blk)]
        return copy_to(mine, mine, g1_send, g1_recv, c, d)

    def g2_copy(c, d):
        start = (down if d == 0 else up) * blk + (0 if d == 0 else hb)
        half = out_buf.at[c, pl.ds(start, hb)]
        return copy_to(half, half, g2_send, g2_recv, c, d)

    def out_copy(c):
        return pltpu.make_async_copy(out_buf.at[c], out_hbm.at[:, :, lanes(c)], out_sem.at[c])

    def stage1(c):
        for d in range(2):
            s1_copy(c, d).start()

    def stage2(c):
        for d in range(2):
            s1_copy(c, d).wait_recv()
            start = (up if d == 0 else down) * blk + (0 if d == 0 else hb)

            def body(i, carry, d=d, start=start):
                sums[c, start + i] = sums[c, start + i] + r1[d, c, i]
                return carry

            lax.fori_loop(0, hb, body, 0)
            s2_copy(c, d).start()

    def stage3(c):
        for d in range(2):
            s2_copy(c, d).wait_recv()

        def body(i, carry):
            z = me_v * blk + i
            merged = sums[c, z] + (r2[0, c, i] + r2[1, c, i])
            out_buf[c, z] = est_ext[c, z, pl.ds(pad, ny), :] * merged / count
            return carry

        lax.fori_loop(0, blk, body, 0)
        for d in range(2):
            g1_copy(c, d).start()

    def stage4(c):
        for d in range(2):
            g1_copy(c, d).wait_recv()
            g2_copy(c, d).start()

    def stage5(c):
        for d in range(2):
            g2_copy(c, d).wait_recv()
        out_copy(c).start()

    stages = (stage1, stage2, stage3, stage4, stage5)

    def tick(k):
        for n, stage in enumerate(stages):
            if 0 <= k - n < chunks:
                stage(k - n)

    for c in range(chunks):
        quotient(c)
        back_yz(c)
        if c >= 1:
            back_x(c - 1)
            tick(c - 1)
    back_x(chunks - 1)
    for k in range(chunks - 1, chunks + len(stages) - 1):
        tick(k)

    for c in range(chunks):
        sent = reg.at[c, pl.ds(0, nz - planes)]
        pltpu.make_async_copy(sent, sent, a2a_send.at[c]).wait()
        for d in range(2):
            s1_copy(c, d).wait_send()
            s2_copy(c, d).wait_send()
            g1_copy(c, d).wait_send()
            g2_copy(c, d).wait_send()
        out_copy(c).wait()

    @pl.when(has_left)
    def _():
        for c in range(chunks):
            est_copy(c, 0).wait_send()
            qh_copy(c, 0).wait_send()

    @pl.when(has_right)
    def _():
        for c in range(chunks):
            est_copy(c, 1).wait_send()
            qh_copy(c, 1).wait_send()


def solution(mesh):
    nv, nt = mesh.shape["view"], mesh.shape["tile"]

    def on_device(estimate, view_stacks, profile_z, profile_y, profile_x, offsets, coverage):
        nz, ny, nx = estimate.shape
        kz, ky, kx = profile_z.shape[1], profile_y.shape[1], profile_x.shape[1]
        planes = view_stacks.shape[1]
        tx = 4 if nt == 32 else 2
        chunks = nx // LANES
        pad = 8
        half_y = ky // 2
        blk = nz // nv
        hb = blk // 2
        dims = (nv, nt, tx, nz, ny, nx, kz, ky, kx)
        any_spec = pl.BlockSpec(memory_space=pl.ANY)
        smem_spec = pl.BlockSpec(memory_space=pltpu.SMEM)
        dma = pltpu.SemaphoreType.DMA
        return pl.pallas_call(
            functools.partial(rl_kernel, dims),
            out_shape=jax.ShapeDtypeStruct(estimate.shape, F32),
            in_specs=[any_spec, any_spec] + [smem_spec] * 5,
            out_specs=any_spec,
            scratch_shapes=[
                pltpu.VMEM(view_stacks.shape[1:], F32),
                pltpu.VMEM((chunks, nz, ny, LANES), F32),
                pltpu.VMEM((chunks, nz, ny + 2 * pad, LANES), F32),
                pltpu.VMEM((ny + 2 * half_y, nz, nx), F32),
                pltpu.VMEM((ny + 2 * half_y, nz, nx), F32),
                pltpu.VMEM((ny, nz, nx), F32),
                pltpu.VMEM((2, chunks, hb, ny, LANES), F32),
                pltpu.VMEM((2, chunks, blk, ny, LANES), F32),
                pltpu.VMEM((chunks, nz, ny, LANES), F32),
                pltpu.VMEM((nz, 2 * LANES), F32),
                pltpu.VMEM((2 * nz, 2 * nz), BF16),
                pltpu.VMEM((2 * nz, 2 * nz), BF16),
                pltpu.VMEM((3 * LANES, 2 * LANES), BF16),
                pltpu.VMEM((3 * LANES, 2 * LANES), BF16),
                dma,
                dma((chunks,)),
                dma((chunks,)),
                dma((chunks, 2)),
                dma((chunks, 2)),
                dma((chunks,)),
                dma((chunks,)),
            ]
            + [dma((chunks, 2))] * 10
            + [dma((chunks,))],
            compiler_params=pltpu.CompilerParams(
                collective_id=0, has_side_effects=True, vmem_limit_bytes=67_000_000
            ),
        )(estimate, view_stacks, profile_z, profile_y, profile_x, offsets, coverage)

    return jax.shard_map(
        on_device,
        mesh=mesh,
        in_specs=(
            P(None, "tile", None),
            P("view", "tile", None, None),
            P("view", None),
            P("view", None),
            P("view", None),
            P("view"),
            P("tile", None),
        ),
        out_specs=P(None, "tile", None),
        check_vma=False,
    )
```

```python
import functools

import jax
import jax.numpy as jnp
from jax import lax
from jax.experimental import pallas as pl
from jax.experimental.pallas import tpu as pltpu
from jax.sharding import PartitionSpec as P

MESH = pl.DeviceIdType.MESH
CORES = 2
LANES = 128
UNITS = 2
F32 = jnp.float32
BF16 = jnp.bfloat16


def rl_kernel(
    dims,
    est_hbm,
    stack_hbm,
    pz_ref,
    py_ref,
    px_ref,
    off_ref,
    cov_ref,
    out_hbm,
    slab,
    reg,
    est_ext,
    zb,
    q_ext,
    part,
    r1,
    r2,
    out_buf,
    yq,
    az,
    azt,
    wx,
    wxt,
    slab_sem,
    est_load,
    own_sem,
    est_send,
    est_recv,
    a2a_send,
    a2a_recv,
    qh_send,
    qh_recv,
    s1_send,
    s1_recv,
    s2_send,
    s2_recv,
    g1_send,
    g1_recv,
    g2_send,
    g2_recv,
    out_sem,
):
    nv, nt, tx, nz, ny, nx, kz, ky, kx = dims
    planes = nz // nt
    chunks = nx // LANES
    half_y = ky // 2
    half_z = kz // 2
    half_x = kx // 2
    pad = 8
    tz = nt // (tx * CORES)
    blk = nz // nv
    units = UNITS
    sub = blk // units
    half = sub // 2

    me_v = lax.axis_index("view")
    me_t = lax.axis_index("tile")
    up = lax.rem(me_v + 1, nv)
    down = lax.rem(me_v + nv - 1, nv)
    across = lax.rem(me_v + 2, nv)
    core = lax.rem(me_t, CORES)
    at_x = lax.rem(me_t // CORES, tx)
    at_z = me_t // (CORES * tx)

    def at(v, t):
        return {"view": v, "tile": t}

    def tile_at(dz, dx, dc):
        c = lax.rem(core + dc, CORES)
        x = lax.rem(at_x + dx, tx)
        z = lax.rem(at_z + dz, tz)
        return (z * tx + x) * CORES + c

    def peer(k):
        return tile_at(k // (CORES * tx), lax.rem(k // CORES, tx), lax.rem(k, CORES))

    toward = jnp.where(core == 0, tx - 1, 1)
    away = tx - toward
    half_ring = tx // 2

    def free_peer(i):
        dx = away * lax.rem(i // CORES, 2)
        return tile_at(i // (2 * CORES), dx, lax.rem(i, CORES))

    def shared_peer(i):
        dx = jnp.where(lax.rem(i // CORES, 2) == 0, toward, half_ring)
        return tile_at(i // (2 * CORES), dx, lax.rem(i, CORES))

    def lanes(c):
        return pl.ds(c * LANES, LANES)

    def load_est(c):
        return pltpu.make_async_copy(
            est_hbm.at[:, :, lanes(c)], est_ext.at[c, :, pl.ds(pad, ny), :], est_load.at[c]
        )

    load_slab = pltpu.make_async_copy(stack_hbm.at[0], slab, slab_sem)
    load_slab.start()
    for c in range(chunks):
        load_est(c).start()

    barrier = pltpu.get_barrier_semaphore()

    def greet(k, carry):
        pl.semaphore_signal(barrier, inc=1, device_id=at(me_v, peer(k)), device_id_type=MESH)
        return carry

    lax.fori_loop(1, nt, greet, 0)
    for v in (up, down):
        pl.semaphore_signal(barrier, inc=1, device_id=at(v, me_t), device_id_type=MESH)
    pl.semaphore_wait(barrier, nt - 1 + 2)

    def est_copy(c, side):
        target = me_t - 1 if side == 0 else me_t + 1
        rows = pl.ds(0, pad) if side == 0 else pl.ds(ny - pad, pad)
        into = pl.ds(pad + ny, pad) if side == 0 else pl.ds(0, pad)
        return pltpu.make_async_remote_copy(
            src_ref=est_hbm.at[:, rows, lanes(c)],
            dst_ref=est_ext.at[c, :, into, :],
            send_sem=est_send.at[c, side],
            recv_sem=est_recv.at[c, side],
            device_id=at(me_v, lax.rem(target + nt, nt)),
            device_id_type=MESH,
        )

    has_left = me_t > 0
    has_right = me_t < nt - 1

    @pl.when(has_left)
    def _():
        for c in range(chunks):
            est_copy(c, 0).start()

    @pl.when(has_right)
    def _():
        for c in range(chunks):
            est_copy(c, 1).start()

    off = off_ref[0]
    turn = lax.rem(nx - off, nx)
    load_slab.wait()
    rows_block = 64
    lane = lax.broadcasted_iota(jnp.int32, (rows_block, nx), 1) + off
    inside = (lane >= 0) & (lane < nx)
    per_plane = slab.shape[1] // rows_block

    def shift(i, carry):
        p = i // per_plane
        r = pl.ds(pl.multiple_of(lax.rem(i, per_plane) * rows_block, rows_block), rows_block)
        slab[p, r, :] = jnp.where(inside, pltpu.roll(slab[p, r, :], turn, 1), 0.0)
        return carry

    lax.fori_loop(0, planes * per_plane, shift, 0)

    my_planes = pl.ds(me_t * planes, planes)

    def a2a_copy(c, t):
        return pltpu.make_async_remote_copy(
            src_ref=slab.at[:, pl.ds(pl.multiple_of(t * ny, 8), ny), lanes(c)],
            dst_ref=reg.at[c, my_planes],
            send_sem=a2a_send.at[c],
            recv_sem=a2a_recv.at[c],
            device_id=at(me_v, t),
            device_id_type=MESH,
        )

    def send_free(c):
        def send(i, carry):
            a2a_copy(c, free_peer(i)).start()
            return carry

        lax.fori_loop(1, nt // 2, send, 0)

    def send_shared(c):
        def send(i, carry):
            a2a_copy(c, shared_peer(i)).start()
            return carry

        lax.fori_loop(0, nt // 2, send, 0)

    for c in range(2):
        send_shared(c)
        send_free(c)

    def own_planes(c):
        mine = slab.at[:, pl.ds(pl.multiple_of(me_t * ny, 8), ny), lanes(c)]
        return pltpu.make_async_copy(mine, reg.at[c, my_planes], own_sem.at[c])

    for c in range(chunks):
        own_planes(c).start()

    def total(ref, count):
        return lax.fori_loop(1, count, lambda a, s: s + ref[0, a], ref[0, 0])

    def bands(ref, count, gap, scale):
        zero = jnp.zeros(gap.shape, F32)
        full = lax.fori_loop(0, count, lambda a, m: m + jnp.where(gap == a, ref[0, a], 0.0), zero)
        full = full / scale
        hi = full.astype(BF16)
        lo = (full - hi.astype(F32)).astype(BF16)
        return hi, lo

    scale_zy = jnp.full((nz, nz), total(pz_ref, kz), F32) * jnp.full((nz, nz), total(py_ref, ky), F32)
    row = lax.broadcasted_iota(jnp.int32, (nz, nz), 0)
    col = lax.broadcasted_iota(jnp.int32, (nz, nz), 1)
    for ref, gap in ((az, col - row + half_z), (azt, row - col + half_z)):
        hi, lo = bands(pz_ref, kz, gap, scale_zy)
        ref[...] = jnp.concatenate(
            [jnp.concatenate([hi, hi], axis=1), jnp.concatenate([lo, lo], axis=1)], axis=0
        )
    wide = (3 * LANES, LANES)
    scale_x = jnp.full(wide, total(px_ref, kx), F32)
    row = lax.broadcasted_iota(jnp.int32, wide, 0)
    col = lax.broadcasted_iota(jnp.int32, wide, 1) + LANES
    for ref, gap in ((wx, row - col + half_x), (wxt, col - row + half_x)):
        hi, lo = bands(px_ref, kx, gap, scale_x)
        ref[...] = jnp.concatenate([hi, lo], axis=1)

    def split(v):
        hi = v.astype(BF16)
        return hi, (v - hi.astype(F32)).astype(BF16)

    def z_pass(matrix, v):
        hi, lo = split(v)
        r = jnp.dot(matrix[...], jnp.concatenate([hi, lo], axis=0), preferred_element_type=F32)
        return r[:nz] + r[nz:]

    def x_pass(matrix, src, y0, count, c):
        first, last = max(c - 1, 0), min(c + 1, chunks - 1)
        v = src[pl.ds(y0, count), :, first * LANES : (last + 1) * LANES]
        v = v.reshape(count * nz, v.shape[2])
        hi, lo = split(v)
        w = matrix[(first - c + 1) * LANES : (last - c + 2) * LANES, :]
        r = jnp.dot(
            jnp.concatenate([hi, lo], axis=1),
            jnp.concatenate([w, w], axis=0),
            preferred_element_type=F32,
        )
        return r[:, :LANES] + r[:, LANES:]

    for c in range(chunks):
        load_est(c).wait()

    @pl.when(has_left)
    def _():
        for c in range(chunks):
            est_copy(c, 1).wait_recv()

    @pl.when(has_right)
    def _():
        for c in range(chunks):
            est_copy(c, 0).wait_recv()

    rows_ext = ny + 2 * pad

    def clear_edge(start):
        def body(i, carry):
            for c in range(chunks):
                est_ext[c, i, pl.ds(start, pad), :] = jnp.zeros((pad, LANES), F32)
            return carry

        lax.fori_loop(0, nz, body, 0)

    @pl.when(jnp.logical_not(has_left))
    def _():
        clear_edge(0)

    @pl.when(jnp.logical_not(has_right))
    def _():
        clear_edge(pad + ny)

    est_rows = est_ext.reshape(chunks, nz * rows_ext, LANES)
    first_row = pad - half_y

    def blur_z(i, carry):
        rows = pl.ds(i + first_row, nz, stride=rows_ext)
        zb[i] = z_pass(az, jnp.concatenate([est_rows[c, rows, :] for c in range(chunks)], axis=1))
        return carry

    lax.fori_loop(0, ny + 2 * half_y, blur_z, 0)

    zblock = min(32, nz)

    def blur_y(y, carry):
        def inner(j, carry):
            zs = pl.ds(pl.multiple_of(j * zblock, zblock), zblock)
            acc = py_ref[0, 0] * zb[y, zs, :]
            for b in range(1, ky):
                acc = acc + py_ref[0, b] * zb[y + b, zs, :]
            part[y, zs, :] = acc
            return carry

        return lax.fori_loop(0, nz // zblock, inner, carry)

    lax.fori_loop(0, ny, blur_y, 0)

    ygroup = 4

    def blur_x(i, carry):
        y0 = i * ygroup
        for c in range(chunks):
            r = x_pass(wx, part, y0, ygroup, c)
            q_ext[pl.ds(half_y + y0, ygroup), :, lanes(c)] = r.reshape(ygroup, nz, LANES)
        return carry

    lax.fori_loop(0, ny // ygroup, blur_x, 0)

    halo = jnp.zeros((half_y, nz, nx), F32)

    @pl.when(jnp.logical_not(has_left))
    def _():
        q_ext[pl.ds(0, half_y)] = halo

    @pl.when(jnp.logical_not(has_right))
    def _():
        q_ext[pl.ds(half_y + ny, half_y)] = halo

    cov = jnp.full((nz, LANES), cov_ref[0, me_v].astype(F32), F32)
    count = cov_ref[0, 0]
    for v in range(1, nv):
        count = count + cov_ref[0, v]
    count = jnp.full((ny, LANES), count.astype(F32), F32)

    for c in range(chunks):
        own_planes(c).wait()
    reg_rows = reg.reshape(chunks, nz * ny, LANES)

    def qh_copy(c, side):
        target = me_t - 1 if side == 0 else me_t + 1
        rows = pl.ds(half_y, half_y) if side == 0 else pl.ds(ny, half_y)
        into = pl.ds(half_y + ny, half_y) if side == 0 else pl.ds(0, half_y)
        return pltpu.make_async_remote_copy(
            src_ref=q_ext.at[rows, :, lanes(c)],
            dst_ref=q_ext.at[into, :, lanes(c)],
            send_sem=qh_send.at[c, side],
            recv_sem=qh_recv.at[c, side],
            device_id=at(me_v, lax.rem(target + nt, nt)),
            device_id_type=MESH,
        )

    def quotient(c):
        arrived = reg.at[c, pl.ds(0, nz - planes)]
        pltpu.make_async_copy(arrived, arrived, a2a_recv.at[c]).wait()

        def body(y, carry):
            v = reg_rows[c, pl.ds(y, nz, stride=ny), :]
            q_ext[half_y + y, :, lanes(c)] = v / q_ext[half_y + y, :, lanes(c)]
            return carry

        lax.fori_loop(0, ny, body, 0)

        @pl.when(has_left)
        def _():
            qh_copy(c, 0).start()

        @pl.when(has_right)
        def _():
            qh_copy(c, 1).start()

    def back_yz(c):
        @pl.when(has_left)
        def _():
            qh_copy(c, 1).wait_recv()

        @pl.when(has_right)
        def _():
            qh_copy(c, 0).wait_recv()

        def body(i, carry):
            for k in range(2):
                acc = py_ref[0, ky - 1] * q_ext[2 * i + k, :, lanes(c)]
                for b in range(1, ky):
                    acc = acc + py_ref[0, ky - 1 - b] * q_ext[2 * i + k + b, :, lanes(c)]
                yq[:, k * LANES : (k + 1) * LANES] = acc
            r = z_pass(azt, yq[...])
            for k in range(2):
                zb[2 * i + k, :, lanes(c)] = r[:, k * LANES : (k + 1) * LANES]
            return carry

        lax.fori_loop(0, ny // 2, body, 0)

    sums = reg

    def back_x(c):
        def body(i, carry):
            r = x_pass(wxt, zb, i * ygroup, ygroup, c).reshape(ygroup, nz, LANES)
            for k in range(ygroup):
                reg_rows[c, pl.ds(i * ygroup + k, nz, stride=ny), :] = cov * r[k]
            return carry

        lax.fori_loop(0, ny // ygroup, body, 0)

    def copy_to(src, dst, send, recv, c, u, d):
        return pltpu.make_async_remote_copy(
            src_ref=src,
            dst_ref=dst,
            send_sem=send.at[c, u, d],
            recv_sem=recv.at[c, u, d],
            device_id=at(up if d == 0 else down, me_t),
            device_id_type=MESH,
        )

    def s1_copy(c, u, d):
        start = across * blk + u * sub + (0 if d == 0 else half)
        return copy_to(sums.at[c, pl.ds(start, half)], r1.at[d, c, u], s1_send, s1_recv, c, u, d)

    def s2_copy(c, u, d):
        start = (up if d == 0 else down) * blk + u * sub
        return copy_to(sums.at[c, pl.ds(start, sub)], r2.at[d, c, u], s2_send, s2_recv, c, u, d)

    def g1_copy(c, u, d):
        mine = out_buf.at[c, pl.ds(me_v * blk + u * sub, sub)]
        return copy_to(mine, mine, g1_send, g1_recv, c, u, d)

    def g2_copy(c, u, d):
        start = (down if d == 0 else up) * blk + u * sub + (0 if d == 0 else half)
        piece = out_buf.at[c, pl.ds(start, half)]
        return copy_to(piece, piece, g2_send, g2_recv, c, u, d)

    def out_copy(c):
        return pltpu.make_async_copy(out_buf.at[c], out_hbm.at[:, :, lanes(c)], out_sem.at[c])

    def stage1(c):
        for u in range(units):
            for d in range(2):
                s1_copy(c, u, d).start()

    def stage2(c):
        for u in range(units):
            for d in range(2):
                s1_copy(c, u, d).wait_recv()
                start = (up if d == 0 else down) * blk + u * sub + (0 if d == 0 else half)

                def body(i, carry, u=u, d=d, start=start):
                    sums[c, start + i] = sums[c, start + i] + r1[d, c, u, i]
                    return carry

                lax.fori_loop(0, half, body, 0)
                s2_copy(c, u, d).start()

    def stage3(c):
        for u in range(units):
            for d in range(2):
                s2_copy(c, u, d).wait_recv()

            def body(i, carry, u=u):
                z = me_v * blk + u * sub + i
                merged = sums[c, z] + (r2[0, c, u, i] + r2[1, c, u, i])
                out_buf[c, z] = est_ext[c, z, pl.ds(pad, ny), :] * merged / count
                return carry

            lax.fori_loop(0, sub, body, 0)
            for d in range(2):
                g1_copy(c, u, d).start()

    def stage4(c):
        for u in range(units):
            for d in range(2):
                g1_copy(c, u, d).wait_recv()
                g2_copy(c, u, d).start()

    def stage5(c):
        for u in range(units):
            for d in range(2):
                g2_copy(c, u, d).wait_recv()
        out_copy(c).start()

    quotient(0)
    send_free(2)
    quotient(1)
    send_shared(2)
    send_free(3)
    back_yz(0)
    back_yz(1)
    back_x(0)
    stage1(0)
    stage2(0)
    quotient(2)
    send_shared(3)
    stage3(0)
    back_yz(2)
    back_x(1)
    stage1(1)
    stage4(0)
    stage2(1)
    quotient(3)
    stage3(1)
    back_yz(3)
    back_x(2)
    stage1(2)
    back_x(3)
    stage1(3)
    stage5(0)
    stage4(1)
    stage2(2)
    stage2(3)
    stage3(2)
    stage5(1)
    stage3(3)
    stage4(2)
    stage4(3)
    stage5(2)
    stage5(3)

    for c in range(chunks):
        sent = reg.at[c, pl.ds(0, nz - planes)]
        pltpu.make_async_copy(sent, sent, a2a_send.at[c]).wait()
        for u in range(units):
            for d in range(2):
                s1_copy(c, u, d).wait_send()
                s2_copy(c, u, d).wait_send()
                g1_copy(c, u, d).wait_send()
                g2_copy(c, u, d).wait_send()
        out_copy(c).wait()

    @pl.when(has_left)
    def _():
        for c in range(chunks):
            est_copy(c, 0).wait_send()
            qh_copy(c, 0).wait_send()

    @pl.when(has_right)
    def _():
        for c in range(chunks):
            est_copy(c, 1).wait_send()
            qh_copy(c, 1).wait_send()


def solution(mesh):
    nv, nt = mesh.shape["view"], mesh.shape["tile"]

    def on_device(estimate, view_stacks, profile_z, profile_y, profile_x, offsets, coverage):
        nz, ny, nx = estimate.shape
        kz, ky, kx = profile_z.shape[1], profile_y.shape[1], profile_x.shape[1]
        planes = view_stacks.shape[1]
        tx = 4 if nt == 32 else 2
        chunks = nx // LANES
        pad = 8
        half_y = ky // 2
        blk = nz // nv
        sub = blk // UNITS
        dims = (nv, nt, tx, nz, ny, nx, kz, ky, kx)
        any_spec = pl.BlockSpec(memory_space=pl.ANY)
        smem_spec = pl.BlockSpec(memory_space=pltpu.SMEM)
        dma = pltpu.SemaphoreType.DMA
        return pl.pallas_call(
            functools.partial(rl_kernel, dims),
            out_shape=jax.ShapeDtypeStruct(estimate.shape, F32),
            in_specs=[any_spec, any_spec] + [smem_spec] * 5,
            out_specs=any_spec,
            scratch_shapes=[
                pltpu.VMEM(view_stacks.shape[1:], F32),
                pltpu.VMEM((chunks, nz, ny, LANES), F32),
                pltpu.VMEM((chunks, nz, ny + 2 * pad, LANES), F32),
                pltpu.VMEM((ny + 2 * half_y, nz, nx), F32),
                pltpu.VMEM((ny + 2 * half_y, nz, nx), F32),
                pltpu.VMEM((ny, nz, nx), F32),
                pltpu.VMEM((2, chunks, UNITS, sub // 2, ny, LANES), F32),
                pltpu.VMEM((2, chunks, UNITS, sub, ny, LANES), F32),
                pltpu.VMEM((chunks, nz, ny, LANES), F32),
                pltpu.VMEM((nz, 2 * LANES), F32),
                pltpu.VMEM((2 * nz, 2 * nz), BF16),
                pltpu.VMEM((2 * nz, 2 * nz), BF16),
                pltpu.VMEM((3 * LANES, 2 * LANES), BF16),
                pltpu.VMEM((3 * LANES, 2 * LANES), BF16),
                dma,
                dma((chunks,)),
                dma((chunks,)),
                dma((chunks, 2)),
                dma((chunks, 2)),
                dma((chunks,)),
                dma((chunks,)),
            ]
            + [dma((chunks, 2))] * 2
            + [dma((chunks, UNITS, 2))] * 8
            + [dma((chunks,))],
            compiler_params=pltpu.CompilerParams(
                collective_id=0, has_side_effects=True, vmem_limit_bytes=67_000_000
            ),
        )(estimate, view_stacks, profile_z, profile_y, profile_x, offsets, coverage)

    return jax.shard_map(
        on_device,
        mesh=mesh,
        in_specs=(
            P(None, "tile", None),
            P("view", "tile", None, None),
            P("view", None),
            P("view", None),
            P("view", None),
            P("view"),
            P("tile", None),
        ),
        out_specs=P(None, "tile", None),
        check_vma=False,
    )
```

```python
import functools

import jax
import jax.numpy as jnp
from jax import lax
from jax.experimental import pallas as pl
from jax.experimental.pallas import tpu as pltpu
from jax.sharding import PartitionSpec as P

MESH = pl.DeviceIdType.MESH
CORES = 2
LANES = 128
UNITS = 2
F32 = jnp.float32
BF16 = jnp.bfloat16


def rl_kernel(
    dims,
    est_hbm,
    stack_hbm,
    pz_ref,
    py_ref,
    px_ref,
    off_ref,
    cov_ref,
    out_buf,
    slab,
    reg,
    est_ext,
    zb,
    q_ext,
    part,
    r1,
    r2,
    yq,
    az,
    azt,
    wx,
    wxt,
    slab_sem,
    est_load,
    own_sem,
    inner_send,
    inner_recv,
    outer_send,
    outer_recv,
    pass_send,
    pass_recv,
    a2a_send,
    a2a_recv,
    qh_send,
    qh_recv,
    s1_send,
    s1_recv,
    s2_send,
    s2_recv,
    g1_send,
    g1_recv,
    g2_send,
    g2_recv,
):
    nv, nt, tx, nz, ny, nx, kz, ky, kx = dims
    planes = nz // nt
    chunks = nx // LANES
    half_y = ky // 2
    half_z = kz // 2
    half_x = kx // 2
    pad = 8
    tz = nt // (tx * CORES)
    blk = nz // nv
    units = UNITS
    sub = blk // units
    half = sub // 2

    me_v = lax.axis_index("view")
    me_t = lax.axis_index("tile")
    up = lax.rem(me_v + 1, nv)
    down = lax.rem(me_v + nv - 1, nv)
    across = lax.rem(me_v + 2, nv)
    core = lax.rem(me_t, CORES)
    at_x = lax.rem(me_t // CORES, tx)
    at_z = me_t // (CORES * tx)

    def at(v, t):
        return {"view": v, "tile": t}

    def tile_at(dz, dx, dc):
        c = lax.rem(core + dc, CORES)
        x = lax.rem(at_x + dx, tx)
        z = lax.rem(at_z + dz, tz)
        return (z * tx + x) * CORES + c

    def peer(k):
        return tile_at(k // (CORES * tx), lax.rem(k // CORES, tx), lax.rem(k, CORES))

    toward = jnp.where(core == 0, tx - 1, 1)
    away = tx - toward
    half_ring = tx // 2

    def free_peer(i):
        dx = away * lax.rem(i // CORES, 2)
        return tile_at(i // (2 * CORES), dx, lax.rem(i, CORES))

    def shared_peer(i):
        dx = jnp.where(lax.rem(i // CORES, 2) == 0, toward, half_ring)
        return tile_at(i // (2 * CORES), dx, lax.rem(i, CORES))

    def lanes(c):
        return pl.ds(c * LANES, LANES)

    def load_slab(p):
        return pltpu.make_async_copy(stack_hbm.at[0, p], slab.at[p], slab_sem.at[p])

    def load_est(c):
        return pltpu.make_async_copy(
            est_hbm.at[:, :, lanes(c)], est_ext.at[c, :, pl.ds(pad, ny), :], est_load.at[c]
        )

    for p in range(planes):
        load_slab(p).start()
    for c in range(chunks):
        load_est(c).start()

    barrier = pltpu.get_barrier_semaphore()

    def greet(k, carry):
        pl.semaphore_signal(barrier, inc=1, device_id=at(me_v, peer(k)), device_id_type=MESH)
        return carry

    lax.fori_loop(1, nt, greet, 0)
    for v in (up, down):
        pl.semaphore_signal(barrier, inc=1, device_id=at(v, me_t), device_id_type=MESH)
    pl.semaphore_wait(barrier, nt - 1 + 2)

    has_left = me_t > 0
    has_right = me_t < nt - 1
    has_outer = jnp.where(core == 0, me_t, nt - 1 - me_t) > 0

    def aligned(row):
        return pl.ds(pl.multiple_of(row, 8), pad)

    def inner_copy(c):
        return pltpu.make_async_remote_copy(
            src_ref=est_hbm.at[:, aligned((1 - core) * (ny - pad)), lanes(c)],
            dst_ref=est_ext.at[c, :, aligned(core * (ny + pad)), :],
            send_sem=inner_send.at[c],
            recv_sem=inner_recv.at[c],
            device_id=at(me_v, me_t + 1 - 2 * core),
            device_id_type=MESH,
        )

    def outer_copy(c):
        share = pl.ds(me_v * blk, blk)
        return pltpu.make_async_remote_copy(
            src_ref=est_hbm.at[share, aligned(core * (ny - pad)), lanes(c)],
            dst_ref=est_ext.at[c, share, aligned((1 - core) * (ny + pad)), :],
            send_sem=outer_send.at[c],
            recv_sem=outer_recv.at[c],
            device_id=at(me_v, lax.rem(me_t + nt - 1 + 2 * core, nt)),
            device_id_type=MESH,
        )

    outer_rows = aligned(core * (ny + pad))

    def pass_copy(n, d):
        if n == 0:
            share = pl.ds(me_v * blk, blk)
        else:
            share = pl.ds((down if d == 0 else up) * blk + d * (blk // 2), blk // 2)
        region = est_ext.at[:, share, outer_rows, :]
        return pltpu.make_async_remote_copy(
            src_ref=region,
            dst_ref=region,
            send_sem=pass_send.at[n, d],
            recv_sem=pass_recv.at[n, d],
            device_id=at(up if d == 0 else down, me_t),
            device_id_type=MESH,
        )

    @pl.when(has_outer)
    def _():
        for c in range(chunks):
            outer_copy(c).start()

    for c in range(chunks):
        inner_copy(c).start()

    off = off_ref[0]
    turn = lax.rem(LANES - off, LANES)
    rows_block = 64
    lane = lax.broadcasted_iota(jnp.int32, (rows_block, LANES), 1) + off
    over = lane >= LANES
    under = lane < 0
    nothing = jnp.zeros((rows_block, LANES), F32)

    for p in range(planes):
        load_slab(p).wait()

        def shift(i, carry, p=p):
            r = pl.ds(pl.multiple_of(i * rows_block, rows_block), rows_block)
            v = [nothing] + [pltpu.roll(slab[p, r, lanes(c)], turn, 1) for c in range(chunks)] + [nothing]
            for c in range(chunks):
                slab[p, r, lanes(c)] = jnp.where(over, v[c + 2], jnp.where(under, v[c], v[c + 1]))
            return carry

        lax.fori_loop(0, slab.shape[1] // rows_block, shift, 0)

    my_planes = pl.ds(me_t * planes, planes)

    def a2a_copy(c, t):
        return pltpu.make_async_remote_copy(
            src_ref=slab.at[:, pl.ds(pl.multiple_of(t * ny, 8), ny), lanes(c)],
            dst_ref=reg.at[c, my_planes],
            send_sem=a2a_send.at[c],
            recv_sem=a2a_recv.at[c],
            device_id=at(me_v, t),
            device_id_type=MESH,
        )

    def send_free(c):
        def send(i, carry):
            a2a_copy(c, free_peer(i)).start()
            return carry

        lax.fori_loop(1, nt // 2, send, 0)

    def send_shared(c):
        def send(i, carry):
            a2a_copy(c, shared_peer(i)).start()
            return carry

        lax.fori_loop(0, nt // 2, send, 0)

    for c in range(2):
        send_shared(c)
        send_free(c)

    def own_planes(c):
        mine = slab.at[:, pl.ds(pl.multiple_of(me_t * ny, 8), ny), lanes(c)]
        return pltpu.make_async_copy(mine, reg.at[c, my_planes], own_sem.at[c])

    for c in range(chunks):
        own_planes(c).start()

    def total(ref, count):
        return lax.fori_loop(1, count, lambda a, s: s + ref[0, a], ref[0, 0])

    def bands(ref, count, gap, scale):
        zero = jnp.zeros(gap.shape, F32)
        full = lax.fori_loop(0, count, lambda a, m: m + jnp.where(gap == a, ref[0, a], 0.0), zero)
        full = full / scale
        hi = full.astype(BF16)
        lo = (full - hi.astype(F32)).astype(BF16)
        return hi, lo

    scale_zy = jnp.full((nz, nz), total(pz_ref, kz), F32) * jnp.full((nz, nz), total(py_ref, ky), F32)
    row = lax.broadcasted_iota(jnp.int32, (nz, nz), 0)
    col = lax.broadcasted_iota(jnp.int32, (nz, nz), 1)
    for ref, gap in ((az, col - row + half_z), (azt, row - col + half_z)):
        hi, lo = bands(pz_ref, kz, gap, scale_zy)
        ref[...] = jnp.concatenate(
            [jnp.concatenate([hi, hi], axis=1), jnp.concatenate([lo, lo], axis=1)], axis=0
        )
    wide = (3 * LANES, LANES)
    scale_x = jnp.full(wide, total(px_ref, kx), F32)
    row = lax.broadcasted_iota(jnp.int32, wide, 0)
    col = lax.broadcasted_iota(jnp.int32, wide, 1) + LANES
    for ref, gap in ((wx, row - col + half_x), (wxt, col - row + half_x)):
        hi, lo = bands(px_ref, kx, gap, scale_x)
        ref[...] = jnp.concatenate([hi, lo], axis=1)

    def split(v):
        hi = v.astype(BF16)
        return hi, (v - hi.astype(F32)).astype(BF16)

    def z_pass(matrix, v):
        hi, lo = split(v)
        r = jnp.dot(matrix[...], jnp.concatenate([hi, lo], axis=0), preferred_element_type=F32)
        return r[:nz] + r[nz:]

    def x_pass(matrix, src, y0, count, c):
        first, last = max(c - 1, 0), min(c + 1, chunks - 1)
        v = src[pl.ds(y0, count), :, first * LANES : (last + 1) * LANES]
        v = v.reshape(count * nz, v.shape[2])
        hi, lo = split(v)
        w = matrix[(first - c + 1) * LANES : (last - c + 2) * LANES, :]
        r = jnp.dot(
            jnp.concatenate([hi, lo], axis=1),
            jnp.concatenate([w, w], axis=0),
            preferred_element_type=F32,
        )
        return r[:, :LANES] + r[:, LANES:]

    rows_ext = ny + 2 * pad
    est_rows = est_ext.reshape(chunks, nz * rows_ext, LANES)
    first_row = pad - half_y

    def blur_z(i, carry):
        rows = pl.ds(i + first_row, nz, stride=rows_ext)
        zb[i] = z_pass(az, jnp.concatenate([est_rows[c, rows, :] for c in range(chunks)], axis=1))
        return carry

    zblock = min(32, nz)

    def blur_y(y, carry):
        def inner(j, carry):
            zs = pl.ds(pl.multiple_of(j * zblock, zblock), zblock)
            acc = py_ref[0, 0] * zb[y, zs, :]
            for b in range(1, ky):
                acc = acc + py_ref[0, b] * zb[y + b, zs, :]
            part[y, zs, :] = acc
            return carry

        return lax.fori_loop(0, nz // zblock, inner, carry)

    ygroup = 4

    def blur_x(cs):
        def body(i, carry):
            y0 = i * ygroup
            for c in cs:
                r = x_pass(wx, part, y0, ygroup, c)
                q_ext[pl.ds(half_y + y0, ygroup), :, lanes(c)] = r.reshape(ygroup, nz, LANES)
            return carry

        return body

    @pl.when(has_outer)
    def _():
        for c in range(chunks):
            outer_copy(c).wait_recv()
        for d in range(2):
            pass_copy(0, d).start()

    @pl.when(jnp.logical_not(has_outer))
    def _():
        def body(i, carry):
            for c in range(chunks):
                est_ext[c, i, outer_rows, :] = jnp.zeros((pad, LANES), F32)
            return carry

        lax.fori_loop(0, nz, body, 0)

    for c in range(chunks):
        load_est(c).wait()
    lax.fori_loop(half_y, half_y + ny, blur_z, 0)
    lax.fori_loop(pad, ny - pad, blur_y, 0)

    @pl.when(has_outer)
    def _():
        for d in range(2):
            pass_copy(0, d).wait_recv()
            pass_copy(1, d).start()

    lax.fori_loop(pad // ygroup, (ny - pad) // ygroup, blur_x(range(chunks)), 0)
    for c in range(chunks):
        inner_copy(c).wait_recv()

    @pl.when(has_outer)
    def _():
        for d in range(2):
            pass_copy(1, d).wait_recv()

    for first, last in ((0, half_y), (half_y + ny, ny + 2 * half_y)):
        lax.fori_loop(first, last, blur_z, 0)
    for first, last in ((0, pad), (ny - pad, ny)):
        lax.fori_loop(first, last, blur_y, 0)

    def blur_x_rest(cs):
        for first, last in ((0, pad), (ny - pad, ny)):
            lax.fori_loop(first // ygroup, last // ygroup, blur_x(cs), 0)

    blur_x_rest((0, 1))

    halo = jnp.zeros((half_y, nz, nx), F32)

    @pl.when(jnp.logical_not(has_left))
    def _():
        q_ext[pl.ds(0, half_y)] = halo

    @pl.when(jnp.logical_not(has_right))
    def _():
        q_ext[pl.ds(half_y + ny, half_y)] = halo

    cov = jnp.full((nz, LANES), cov_ref[0, me_v].astype(F32), F32)
    count = cov_ref[0, 0]
    for v in range(1, nv):
        count = count + cov_ref[0, v]
    count = jnp.full((ny, LANES), count.astype(F32), F32)

    for c in range(chunks):
        own_planes(c).wait()
    reg_rows = reg.reshape(chunks, nz * ny, LANES)

    def qh_copy(c, side):
        target = me_t - 1 if side == 0 else me_t + 1
        rows = pl.ds(half_y, half_y) if side == 0 else pl.ds(ny, half_y)
        into = pl.ds(half_y + ny, half_y) if side == 0 else pl.ds(0, half_y)
        return pltpu.make_async_remote_copy(
            src_ref=q_ext.at[rows, :, lanes(c)],
            dst_ref=q_ext.at[into, :, lanes(c)],
            send_sem=qh_send.at[c, side],
            recv_sem=qh_recv.at[c, side],
            device_id=at(me_v, lax.rem(target + nt, nt)),
            device_id_type=MESH,
        )

    def quotient(c):
        arrived = reg.at[c, pl.ds(0, nz - planes)]
        pltpu.make_async_copy(arrived, arrived, a2a_recv.at[c]).wait()

        def body(y, carry):
            v = reg_rows[c, pl.ds(y, nz, stride=ny), :]
            q_ext[half_y + y, :, lanes(c)] = v / q_ext[half_y + y, :, lanes(c)]
            return carry

        lax.fori_loop(0, ny, body, 0)

        @pl.when(has_left)
        def _():
            qh_copy(c, 0).start()

        @pl.when(has_right)
        def _():
            qh_copy(c, 1).start()

    def back_pairs(c, first, last):
        def body(i, carry):
            for k in range(2):
                acc = py_ref[0, ky - 1] * q_ext[2 * i + k, :, lanes(c)]
                for b in range(1, ky):
                    acc = acc + py_ref[0, ky - 1 - b] * q_ext[2 * i + k + b, :, lanes(c)]
                yq[:, k * LANES : (k + 1) * LANES] = acc
            r = z_pass(azt, yq[...])
            for k in range(2):
                zb[2 * i + k, :, lanes(c)] = r[:, k * LANES : (k + 1) * LANES]
            return carry

        lax.fori_loop(first // 2, last // 2, body, 0)

    def back_inner(c):
        back_pairs(c, pad, ny - pad)

    def back_outer(c):
        @pl.when(has_left)
        def _():
            qh_copy(c, 1).wait_recv()

        @pl.when(has_right)
        def _():
            qh_copy(c, 0).wait_recv()

        back_pairs(c, 0, pad)
        back_pairs(c, ny - pad, ny)

    sums = reg

    def back_x(c):
        def body(i, carry):
            r = x_pass(wxt, zb, i * ygroup, ygroup, c).reshape(ygroup, nz, LANES)
            for k in range(ygroup):
                reg_rows[c, pl.ds(i * ygroup + k, nz, stride=ny), :] = cov * r[k]
            return carry

        lax.fori_loop(0, ny // ygroup, body, 0)

    def copy_to(src, dst, send, recv, c, u, d):
        return pltpu.make_async_remote_copy(
            src_ref=src,
            dst_ref=dst,
            send_sem=send.at[c, u, d],
            recv_sem=recv.at[c, u, d],
            device_id=at(up if d == 0 else down, me_t),
            device_id_type=MESH,
        )

    def s1_copy(c, u, d):
        start = across * blk + u * sub + (0 if d == 0 else half)
        return copy_to(sums.at[c, pl.ds(start, half)], r1.at[d, c, u], s1_send, s1_recv, c, u, d)

    def s2_copy(c, u, d):
        start = (up if d == 0 else down) * blk + u * sub
        return copy_to(sums.at[c, pl.ds(start, sub)], r2.at[d, c, u], s2_send, s2_recv, c, u, d)

    def g1_copy(c, u, d):
        mine = out_buf.at[pl.ds(me_v * blk + u * sub, sub), :, lanes(c)]
        return copy_to(mine, mine, g1_send, g1_recv, c, u, d)

    def g2_copy(c, u, d):
        start = (down if d == 0 else up) * blk + u * sub + (0 if d == 0 else half)
        piece = out_buf.at[pl.ds(start, half), :, lanes(c)]
        return copy_to(piece, piece, g2_send, g2_recv, c, u, d)

    def stage1(c):
        for u in range(units):
            for d in range(2):
                s1_copy(c, u, d).start()

    def stage2(c):
        for u in range(units):
            for d in range(2):
                s1_copy(c, u, d).wait_recv()
                start = (up if d == 0 else down) * blk + u * sub + (0 if d == 0 else half)

                def body(i, carry, u=u, d=d, start=start):
                    sums[c, start + i] = sums[c, start + i] + r1[d, c, u, i]
                    return carry

                lax.fori_loop(0, half, body, 0)
                s2_copy(c, u, d).start()

    def stage3(c):
        for u in range(units):
            for d in range(2):
                s2_copy(c, u, d).wait_recv()

            def body(i, carry, u=u):
                z = me_v * blk + u * sub + i
                merged = sums[c, z] + (r2[0, c, u, i] + r2[1, c, u, i])
                out_buf[z, :, lanes(c)] = est_ext[c, z, pl.ds(pad, ny), :] * merged / count
                return carry

            lax.fori_loop(0, sub, body, 0)
            for d in range(2):
                g1_copy(c, u, d).start()

    def stage4(c):
        for u in range(units):
            for d in range(2):
                g1_copy(c, u, d).wait_recv()
                g2_copy(c, u, d).start()

    def stage5(c):
        for u in range(units):
            for d in range(2):
                g2_copy(c, u, d).wait_recv()

    quotient(0)
    send_free(2)
    quotient(1)
    send_shared(2)
    send_free(3)
    back_inner(0)
    back_inner(1)
    back_outer(0)
    back_outer(1)
    back_x(0)
    stage1(0)
    blur_x_rest((2, 3))
    stage2(0)
    quotient(2)
    send_shared(3)
    stage3(0)
    back_inner(2)
    back_outer(2)
    back_x(1)
    stage1(1)
    stage4(0)
    stage2(1)
    quotient(3)
    stage3(1)
    back_inner(3)
    back_outer(3)
    back_x(2)
    stage1(2)
    back_x(3)
    stage1(3)
    stage5(0)
    stage4(1)
    stage2(2)
    stage2(3)
    stage3(2)
    stage5(1)
    stage3(3)
    stage4(2)
    stage4(3)
    stage5(2)
    stage5(3)

    for c in range(chunks):
        sent = reg.at[c, pl.ds(0, nz - planes)]
        pltpu.make_async_copy(sent, sent, a2a_send.at[c]).wait()
        for u in range(units):
            for d in range(2):
                s1_copy(c, u, d).wait_send()
                s2_copy(c, u, d).wait_send()
                g1_copy(c, u, d).wait_send()
                g2_copy(c, u, d).wait_send()

        inner_copy(c).wait_send()

    @pl.when(has_outer)
    def _():
        for c in range(chunks):
            outer_copy(c).wait_send()
        for n in range(2):
            for d in range(2):
                pass_copy(n, d).wait_send()

    @pl.when(has_left)
    def _():
        for c in range(chunks):
            qh_copy(c, 0).wait_send()

    @pl.when(has_right)
    def _():
        for c in range(chunks):
            qh_copy(c, 1).wait_send()


def solution(mesh):
    nv, nt = mesh.shape["view"], mesh.shape["tile"]

    def on_device(estimate, view_stacks, profile_z, profile_y, profile_x, offsets, coverage):
        nz, ny, nx = estimate.shape
        kz, ky, kx = profile_z.shape[1], profile_y.shape[1], profile_x.shape[1]
        planes = view_stacks.shape[1]
        tx = 4 if nt == 32 else 2
        chunks = nx // LANES
        pad = 8
        half_y = ky // 2
        blk = nz // nv
        sub = blk // UNITS
        dims = (nv, nt, tx, nz, ny, nx, kz, ky, kx)
        any_spec = pl.BlockSpec(memory_space=pl.ANY)
        smem_spec = pl.BlockSpec(memory_space=pltpu.SMEM)
        dma = pltpu.SemaphoreType.DMA
        return pl.pallas_call(
            functools.partial(rl_kernel, dims),
            out_shape=pltpu.VMEM(estimate.shape, F32),
            in_specs=[any_spec, any_spec] + [smem_spec] * 5,
            out_specs=pl.BlockSpec(memory_space=pltpu.VMEM),
            scratch_shapes=[
                pltpu.VMEM(view_stacks.shape[1:], F32),
                pltpu.VMEM((chunks, nz, ny, LANES), F32),
                pltpu.VMEM((chunks, nz, ny + 2 * pad, LANES), F32),
                pltpu.VMEM((ny + 2 * half_y, nz, nx), F32),
                pltpu.VMEM((ny + 2 * half_y, nz, nx), F32),
                pltpu.VMEM((ny, nz, nx), F32),
                pltpu.VMEM((2, chunks, UNITS, sub // 2, ny, LANES), F32),
                pltpu.VMEM((2, chunks, UNITS, sub, ny, LANES), F32),
                pltpu.VMEM((nz, 2 * LANES), F32),
                pltpu.VMEM((2 * nz, 2 * nz), BF16),
                pltpu.VMEM((2 * nz, 2 * nz), BF16),
                pltpu.VMEM((3 * LANES, 2 * LANES), BF16),
                pltpu.VMEM((3 * LANES, 2 * LANES), BF16),
                dma((planes,)),
                dma((chunks,)),
                dma((chunks,)),
                dma((chunks,)),
                dma((chunks,)),
                dma((chunks,)),
                dma((chunks,)),
                dma((2, 2)),
                dma((2, 2)),
                dma((chunks,)),
                dma((chunks,)),
            ]
            + [dma((chunks, 2))] * 2
            + [dma((chunks, UNITS, 2))] * 8,
            compiler_params=pltpu.CompilerParams(
                collective_id=0, has_side_effects=True, vmem_limit_bytes=60_000_000
            ),
        )(estimate, view_stacks, profile_z, profile_y, profile_x, offsets, coverage)

    return jax.shard_map(
        on_device,
        mesh=mesh,
        in_specs=(
            P(None, "tile", None),
            P("view", "tile", None, None),
            P("view", None),
            P("view", None),
            P("view", None),
            P("view"),
            P("tile", None),
        ),
        out_specs=P(None, "tile", None),
        check_vma=False,
    )
```

```python
import functools

import jax
import jax.numpy as jnp
from jax import lax
from jax.experimental import pallas as pl
from jax.experimental.pallas import tpu as pltpu
from jax.sharding import PartitionSpec as P

MESH = pl.DeviceIdType.MESH
CORES = 2
LANES = 128
UNITS = 2
STRIP = 8
F32 = jnp.float32
BF16 = jnp.bfloat16


def rl_kernel(
    dims,
    est_hbm,
    stack_hbm,
    pz_ref,
    py_ref,
    px_ref,
    off_ref,
    cov_ref,
    out_buf,
    slab,
    reg,
    est_ext,
    zb,
    q_ext,
    part,
    r1,
    r2,
    yq,
    az,
    azt,
    wx,
    wxt,
    wm,
    strip,
    strip_out,
    r1s,
    r2s,
    slab_sem,
    est_load,
    own_sem,
    inner_send,
    inner_recv,
    outer_send,
    outer_recv,
    pass_send,
    pass_recv,
    a2a_send,
    a2a_recv,
    qh_send,
    qh_recv,
    s1_send,
    s1_recv,
    s2_send,
    s2_recv,
    g1_send,
    g1_recv,
    g2_send,
    g2_recv,
):
    nv, nt, tx, nz, ny, nx, kz, ky, kx = dims
    planes = nz // nt
    chunks = nx // LANES
    half_y = ky // 2
    half_z = kz // 2
    half_x = kx // 2
    pad = 8
    tz = nt // (tx * CORES)
    blk = nz // nv
    units = UNITS
    sub = blk // units
    half = sub // 2
    packed = LANES // STRIP
    strip_planes = nz // packed
    strip_blk = strip_planes // nv

    me_v = lax.axis_index("view")
    me_t = lax.axis_index("tile")
    up = lax.rem(me_v + 1, nv)
    down = lax.rem(me_v + nv - 1, nv)
    across = lax.rem(me_v + 2, nv)
    core = lax.rem(me_t, CORES)
    at_x = lax.rem(me_t // CORES, tx)
    at_z = me_t // (CORES * tx)

    def at(v, t):
        return {"view": v, "tile": t}

    def tile_at(dz, dx, dc):
        c = lax.rem(core + dc, CORES)
        x = lax.rem(at_x + dx, tx)
        z = lax.rem(at_z + dz, tz)
        return (z * tx + x) * CORES + c

    def peer(k):
        return tile_at(k // (CORES * tx), lax.rem(k // CORES, tx), lax.rem(k, CORES))

    toward = jnp.where(core == 0, tx - 1, 1)
    away = tx - toward
    half_ring = tx // 2

    def free_peer(i):
        dx = away * lax.rem(i // CORES, 2)
        return tile_at(i // (2 * CORES), dx, lax.rem(i, CORES))

    def shared_peer(i):
        dx = jnp.where(lax.rem(i // CORES, 2) == 0, toward, half_ring)
        return tile_at(i // (2 * CORES), dx, lax.rem(i, CORES))

    def lanes(c):
        return pl.ds(c * LANES, LANES)

    def load_slab(p):
        return pltpu.make_async_copy(stack_hbm.at[0, p], slab.at[p], slab_sem.at[p])

    def load_est(c):
        return pltpu.make_async_copy(
            est_hbm.at[:, :, lanes(c)], est_ext.at[c, :, pl.ds(pad, ny), :], est_load.at[c]
        )

    for p in range(planes):
        load_slab(p).start()
    for c in range(chunks):
        load_est(c).start()

    barrier = pltpu.get_barrier_semaphore()

    def greet(k, carry):
        pl.semaphore_signal(barrier, inc=1, device_id=at(me_v, peer(k)), device_id_type=MESH)
        return carry

    lax.fori_loop(1, nt, greet, 0)
    for v in (up, down):
        pl.semaphore_signal(barrier, inc=1, device_id=at(v, me_t), device_id_type=MESH)
    pl.semaphore_wait(barrier, nt - 1 + 2)

    has_left = me_t > 0
    has_right = me_t < nt - 1
    has_outer = jnp.where(core == 0, me_t, nt - 1 - me_t) > 0

    def aligned(row):
        return pl.ds(pl.multiple_of(row, 8), pad)

    def inner_copy(c):
        return pltpu.make_async_remote_copy(
            src_ref=est_hbm.at[:, aligned((1 - core) * (ny - pad)), lanes(c)],
            dst_ref=est_ext.at[c, :, aligned(core * (ny + pad)), :],
            send_sem=inner_send.at[c],
            recv_sem=inner_recv.at[c],
            device_id=at(me_v, me_t + 1 - 2 * core),
            device_id_type=MESH,
        )

    def outer_copy(c):
        share = pl.ds(me_v * blk, blk)
        return pltpu.make_async_remote_copy(
            src_ref=est_hbm.at[share, aligned(core * (ny - pad)), lanes(c)],
            dst_ref=est_ext.at[c, share, aligned((1 - core) * (ny + pad)), :],
            send_sem=outer_send.at[c],
            recv_sem=outer_recv.at[c],
            device_id=at(me_v, lax.rem(me_t + nt - 1 + 2 * core, nt)),
            device_id_type=MESH,
        )

    outer_rows = aligned(core * (ny + pad))

    def pass_copy(n, h, d):
        if n == 0:
            share = pl.ds(me_v * blk, blk)
        else:
            share = pl.ds((down if d == 0 else up) * blk + d * (blk // 2), blk // 2)
        region = est_ext.at[pl.ds(h * (chunks // 2), chunks // 2), share, outer_rows, :]
        return pltpu.make_async_remote_copy(
            src_ref=region,
            dst_ref=region,
            send_sem=pass_send.at[n, h, d],
            recv_sem=pass_recv.at[n, h, d],
            device_id=at(up if d == 0 else down, me_t),
            device_id_type=MESH,
        )

    @pl.when(has_outer)
    def _():
        for c in range(chunks):
            outer_copy(c).start()

    for c in range(chunks):
        inner_copy(c).start()

    off = off_ref[0]
    turn = lax.rem(LANES - off, LANES)
    rows_block = 64
    lane = lax.broadcasted_iota(jnp.int32, (rows_block, LANES), 1) + off
    over = lane >= LANES
    under = lane < 0
    nothing = jnp.zeros((rows_block, LANES), F32)

    for p in range(planes):
        load_slab(p).wait()

        def shift(i, carry, p=p):
            r = pl.ds(pl.multiple_of(i * rows_block, rows_block), rows_block)
            v = [nothing] + [pltpu.roll(slab[p, r, lanes(c)], turn, 1) for c in range(chunks)] + [nothing]
            for c in range(chunks):
                slab[p, r, lanes(c)] = jnp.where(over, v[c + 2], jnp.where(under, v[c], v[c + 1]))
            return carry

        lax.fori_loop(0, slab.shape[1] // rows_block, shift, 0)

    my_planes = pl.ds(me_t * planes, planes)

    def a2a_copy(c, t):
        return pltpu.make_async_remote_copy(
            src_ref=slab.at[:, pl.ds(pl.multiple_of(t * ny, 8), ny), lanes(c)],
            dst_ref=reg.at[c, my_planes],
            send_sem=a2a_send.at[c],
            recv_sem=a2a_recv.at[c],
            device_id=at(me_v, t),
            device_id_type=MESH,
        )

    def send_free(c):
        def send(i, carry):
            a2a_copy(c, free_peer(i)).start()
            return carry

        lax.fori_loop(1, nt // 2, send, 0)

    def send_shared(c):
        def send(i, carry):
            a2a_copy(c, shared_peer(i)).start()
            return carry

        lax.fori_loop(0, nt // 2, send, 0)

    send_shared(0)
    send_free(0)
    send_free(1)

    def own_planes(c):
        mine = slab.at[:, pl.ds(pl.multiple_of(me_t * ny, 8), ny), lanes(c)]
        return pltpu.make_async_copy(mine, reg.at[c, my_planes], own_sem.at[c])

    for c in range(chunks):
        own_planes(c).start()

    def total(ref, count):
        return lax.fori_loop(1, count, lambda a, s: s + ref[0, a], ref[0, 0])

    def bands(ref, count, gap, scale):
        zero = jnp.zeros(gap.shape, F32)
        full = lax.fori_loop(0, count, lambda a, m: m + jnp.where(gap == a, ref[0, a], 0.0), zero)
        full = full / scale
        hi = full.astype(BF16)
        lo = (full - hi.astype(F32)).astype(BF16)
        return hi, lo

    scale_zy = jnp.full((nz, nz), total(pz_ref, kz), F32) * jnp.full((nz, nz), total(py_ref, ky), F32)
    row = lax.broadcasted_iota(jnp.int32, (nz, nz), 0)
    col = lax.broadcasted_iota(jnp.int32, (nz, nz), 1)
    for ref, gap in ((az, col - row + half_z), (azt, row - col + half_z)):
        hi, lo = bands(pz_ref, kz, gap, scale_zy)
        ref[...] = jnp.concatenate(
            [jnp.concatenate([hi, hi], axis=1), jnp.concatenate([lo, lo], axis=1)], axis=0
        )
    for ref, taps in ((wx, kx), (wxt, kx), (wm, kx)):
        shape = (ref.shape[0], LANES)
        row = lax.broadcasted_iota(jnp.int32, shape, 0)
        col = lax.broadcasted_iota(jnp.int32, shape, 1)
        if ref is wx:
            gap = row - col - LANES + half_x
        elif ref is wxt:
            gap = col - row + LANES
        else:
            gap = lax.rem(col, STRIP) - row + LANES
        hi, lo = bands(px_ref, taps, gap, jnp.full(shape, total(px_ref, kx), F32))
        ref[...] = jnp.concatenate([hi, lo], axis=1)

    def split(v):
        hi = v.astype(BF16)
        return hi, (v - hi.astype(F32)).astype(BF16)

    def z_pass(matrix, v):
        hi, lo = split(v)
        r = jnp.dot(matrix[...], jnp.concatenate([hi, lo], axis=0), preferred_element_type=F32)
        return r[:nz] + r[nz:]

    def x_pass(matrix, src, y0, count, c, reach):
        first, last = max(c - 1, 0), min(c + reach, chunks - 1)
        v = src[pl.ds(y0, count), :, first * LANES : (last + 1) * LANES]
        v = v.reshape(count * nz, v.shape[2])
        hi, lo = split(v)
        w = matrix[(first - c + 1) * LANES : (last - c + 2) * LANES, :]
        r = jnp.dot(
            jnp.concatenate([hi, lo], axis=1),
            jnp.concatenate([w, w], axis=0),
            preferred_element_type=F32,
        )
        return r[:, :LANES] + r[:, LANES:]

    rows_ext = ny + 2 * pad
    est_rows = est_ext.reshape(chunks, nz * rows_ext, LANES)
    first_row = pad - half_y

    def blur_z(h):
        cs = range(h * chunks // 2, (h + 1) * chunks // 2)
        into = pl.ds(h * nx // 2, nx // 2)

        def body(i, carry):
            rows = pl.ds(i + first_row, nz, stride=rows_ext)
            zb[i, :, into] = z_pass(az, jnp.concatenate([est_rows[c, rows, :] for c in cs], axis=1))
            return carry

        return body

    zblock = min(64, nz)

    def blur_y(h):
        into = pl.ds(h * nx // 2, nx // 2)

        def body(y, carry):
            def inner(j, carry):
                zs = pl.ds(pl.multiple_of(j * zblock, zblock), zblock)
                acc = py_ref[0, 0] * zb[y, zs, into]
                for b in range(1, ky):
                    acc = acc + py_ref[0, b] * zb[y + b, zs, into]
                part[y, zs, into] = acc
                return carry

            return lax.fori_loop(0, nz // zblock, inner, carry)

        return body

    ygroup = 4

    def blur_x(cs):
        def body(i, carry):
            y0 = i * ygroup
            for c in cs:
                r = x_pass(wx, part, y0, ygroup, c, 1)
                q_ext[pl.ds(half_y + y0, ygroup), :, lanes(c)] = r.reshape(ygroup, nz, LANES)
            return carry

        return body

    def pass_on(n, h):
        @pl.when(has_outer)
        def _():
            if n == 0:
                for c in range(h * chunks // 2, (h + 1) * chunks // 2):
                    outer_copy(c).wait_recv()
            for d in range(2):
                if n > 0:
                    pass_copy(n - 1, h, d).wait_recv()
                if n < 2:
                    pass_copy(n, h, d).start()

    pass_on(0, 0)
    pass_on(0, 1)

    @pl.when(jnp.logical_not(has_outer))
    def _():
        def body(i, carry):
            for c in range(chunks):
                est_ext[c, i, outer_rows, :] = jnp.zeros((pad, LANES), F32)
            return carry

        lax.fori_loop(0, nz, body, 0)

    for c in range(chunks):
        load_est(c).wait()
    lax.fori_loop(half_y, half_y + ny, blur_z(0), 0)
    pass_on(1, 0)
    lax.fori_loop(half_y, half_y + ny, blur_z(1), 0)
    pass_on(1, 1)
    for h in range(2):
        lax.fori_loop(pad, ny - pad, blur_y(h), 0)
    lax.fori_loop(pad // ygroup, (ny - pad) // ygroup, blur_x(range(chunks)), 0)

    def blur_edges(h):
        for c in range(h * chunks // 2, (h + 1) * chunks // 2):
            inner_copy(c).wait_recv()
        pass_on(2, h)
        for first, last in ((0, half_y), (half_y + ny, ny + 2 * half_y)):
            lax.fori_loop(first, last, blur_z(h), 0)
        for first, last in ((0, pad), (ny - pad, ny)):
            lax.fori_loop(first, last, blur_y(h), 0)

    def blur_x_rest(cs):
        for first, last in ((0, pad), (ny - pad, ny)):
            lax.fori_loop(first // ygroup, last // ygroup, blur_x(cs), 0)

    blur_edges(0)
    blur_x_rest((0,))

    halo = jnp.zeros((half_y, nz, nx), F32)

    @pl.when(jnp.logical_not(has_left))
    def _():
        q_ext[pl.ds(0, half_y)] = halo

    @pl.when(jnp.logical_not(has_right))
    def _():
        q_ext[pl.ds(half_y + ny, half_y)] = halo

    cov = jnp.full((nz, LANES), cov_ref[0, me_v].astype(F32), F32)
    count = cov_ref[0, 0]
    for v in range(1, nv):
        count = count + cov_ref[0, v]
    count = jnp.full((ny, LANES), count.astype(F32), F32)

    for c in range(chunks):
        own_planes(c).wait()
    reg_rows = reg.reshape(chunks, nz * ny, LANES)

    def qh_copy(c, side):
        target = me_t - 1 if side == 0 else me_t + 1
        rows = pl.ds(half_y, half_y) if side == 0 else pl.ds(ny, half_y)
        into = pl.ds(half_y + ny, half_y) if side == 0 else pl.ds(0, half_y)
        return pltpu.make_async_remote_copy(
            src_ref=q_ext.at[rows, :, lanes(c)],
            dst_ref=q_ext.at[into, :, lanes(c)],
            send_sem=qh_send.at[c, side],
            recv_sem=qh_recv.at[c, side],
            device_id=at(me_v, lax.rem(target + nt, nt)),
            device_id_type=MESH,
        )

    def quotient(c):
        arrived = reg.at[c, pl.ds(0, nz - planes)]
        pltpu.make_async_copy(arrived, arrived, a2a_recv.at[c]).wait()

        def body(y, carry):
            v = reg_rows[c, pl.ds(y, nz, stride=ny), :]
            q_ext[half_y + y, :, lanes(c)] = v / q_ext[half_y + y, :, lanes(c)]
            return carry

        lax.fori_loop(0, ny, body, 0)

        @pl.when(has_left)
        def _():
            qh_copy(c, 0).start()

        @pl.when(has_right)
        def _():
            qh_copy(c, 1).start()

    def back_pairs(c, first, last):
        def body(i, carry):
            for k in range(2):
                acc = py_ref[0, ky - 1] * q_ext[2 * i + k, :, lanes(c)]
                for b in range(1, ky):
                    acc = acc + py_ref[0, ky - 1 - b] * q_ext[2 * i + k + b, :, lanes(c)]
                yq[:, k * LANES : (k + 1) * LANES] = acc
            r = z_pass(azt, yq[...])
            for k in range(2):
                zb[2 * i + k, :, lanes(c)] = r[:, k * LANES : (k + 1) * LANES]
            return carry

        lax.fori_loop(first // 2, last // 2, body, 0)

    def back_inner(c):
        back_pairs(c, pad, ny - pad)

    def back_outer(c):
        @pl.when(has_left)
        def _():
            qh_copy(c, 1).wait_recv()

        @pl.when(has_right)
        def _():
            qh_copy(c, 0).wait_recv()

        back_pairs(c, 0, pad)
        back_pairs(c, ny - pad, ny)

    sums = reg
    strip_rows = strip.reshape(strip_planes * ny, LANES)
    row = lax.broadcasted_iota(jnp.int32, (nz, LANES), 0)
    col = lax.broadcasted_iota(jnp.int32, (nz, LANES), 1)
    in_strip = lax.rem(row, packed) == col // STRIP

    def back_strip():
        def body(i, carry):
            r = x_pass(wm, zb, i * ygroup, ygroup, chunks, 0).reshape(ygroup, nz, LANES)
            for k in range(ygroup):
                v = jnp.where(in_strip, cov * r[k], 0.0)
                v = jnp.sum(v.reshape(strip_planes, packed, LANES), axis=1)
                strip_rows[pl.ds(i * ygroup + k, strip_planes, stride=ny), :] = v
            return carry

        lax.fori_loop(0, ny // ygroup, body, 0)

    def back_x(c):
        def body(i, carry):
            r = x_pass(wxt, zb, i * ygroup, ygroup, c, 0).reshape(ygroup, nz, LANES)
            for k in range(ygroup):
                reg_rows[c, pl.ds(i * ygroup + k, nz, stride=ny), :] = cov * r[k]
            return carry

        lax.fori_loop(0, ny // ygroup, body, 0)

    def copy_to(src, dst, send, recv, c, u, d):
        return pltpu.make_async_remote_copy(
            src_ref=src,
            dst_ref=dst,
            send_sem=send.at[c, u, d],
            recv_sem=recv.at[c, u, d],
            device_id=at(up if d == 0 else down, me_t),
            device_id_type=MESH,
        )

    def shares(c):
        return range(1) if c == chunks else range(units)

    def s1_copy(c, u, d):
        if c == chunks:
            src, dst = strip.at[pl.ds(across * strip_blk + d * (strip_blk // 2), strip_blk // 2)], r1s.at[d]
        else:
            start = across * blk + u * sub + (0 if d == 0 else half)
            src, dst = sums.at[c, pl.ds(start, half)], r1.at[d, c, u]
        return copy_to(src, dst, s1_send, s1_recv, c, u, d)

    def s2_copy(c, u, d):
        owner = up if d == 0 else down
        if c == chunks:
            src, dst = strip.at[pl.ds(owner * strip_blk, strip_blk)], r2s.at[d]
        else:
            src, dst = sums.at[c, pl.ds(owner * blk + u * sub, sub)], r2.at[d, c, u]
        return copy_to(src, dst, s2_send, s2_recv, c, u, d)

    def g1_copy(c, u, d):
        if c == chunks:
            mine = strip_out.at[pl.ds(me_v * strip_blk, strip_blk)]
        else:
            mine = out_buf.at[pl.ds(me_v * blk + u * sub, sub), :, lanes(c)]
        return copy_to(mine, mine, g1_send, g1_recv, c, u, d)

    def g2_copy(c, u, d):
        owner = down if d == 0 else up
        if c == chunks:
            piece = strip_out.at[pl.ds(owner * strip_blk + d * (strip_blk // 2), strip_blk // 2)]
        else:
            start = owner * blk + u * sub + (0 if d == 0 else half)
            piece = out_buf.at[pl.ds(start, half), :, lanes(c)]
        return copy_to(piece, piece, g2_send, g2_recv, c, u, d)

    def stage1(c):
        for u in shares(c):
            for d in range(2):
                s1_copy(c, u, d).start()

    def stage2(c):
        for u in shares(c):
            for d in range(2):
                s1_copy(c, u, d).wait_recv()
                owner = up if d == 0 else down
                if c == chunks:
                    at_plane = pl.ds(owner * strip_blk + d * (strip_blk // 2), strip_blk // 2)
                    strip[at_plane] = strip[at_plane] + r1s[d]
                else:
                    start = owner * blk + u * sub + (0 if d == 0 else half)

                    def body(i, carry, u=u, d=d, start=start):
                        sums[c, start + i] = sums[c, start + i] + r1[d, c, u, i]
                        return carry

                    lax.fori_loop(0, half, body, 0)
                s2_copy(c, u, d).start()

    lane_row = lax.broadcasted_iota(jnp.int32, (ny, LANES), 1)
    own_rows = pl.ds(pad, ny)

    def stage3(c):
        for u in shares(c):
            for d in range(2):
                s2_copy(c, u, d).wait_recv()
            if c == chunks:

                def body(i, carry):
                    z = me_v * strip_blk + i
                    est = jnp.zeros((ny, LANES), F32)
                    for k in range(packed):
                        v = est_ext[chunks - 1, z * packed + k, own_rows, :]
                        v = pltpu.roll(v, (k * STRIP + half_x) % LANES, 1)
                        est = jnp.where(lane_row // STRIP == k, v, est)
                    merged = strip[z] + (r2s[0, i] + r2s[1, i])
                    strip_out[z] = est * merged / count
                    return carry

                lax.fori_loop(0, strip_blk, body, 0)
            else:

                def body(i, carry, u=u):
                    z = me_v * blk + u * sub + i
                    merged = sums[c, z] + (r2[0, c, u, i] + r2[1, c, u, i])
                    est = pltpu.roll(est_ext[c, z, own_rows, :], half_x, 1)
                    if c > 0:
                        before = pltpu.roll(est_ext[c - 1, z, own_rows, :], half_x, 1)
                        est = jnp.where(lane_row < half_x, before, est)
                    out_buf[z, :, lanes(c)] = est * merged / count
                    return carry

                lax.fori_loop(0, sub, body, 0)
            for d in range(2):
                g1_copy(c, u, d).start()

    def stage4(c):
        for u in shares(c):
            for d in range(2):
                g1_copy(c, u, d).wait_recv()
                g2_copy(c, u, d).start()

    def stage5(c):
        for u in shares(c):
            for d in range(2):
                g2_copy(c, u, d).wait_recv()

    def realign(c):
        for u in shares(c):
            for d in range(2):
                g1_copy(c, u, d).wait_send()
                g2_copy(c, u, d).wait_send()
        here = lane_row < LANES - half_x

        def body(i, carry):
            for k in range(packed):
                z = i * packed + k
                v = pltpu.roll(out_buf[z, :, lanes(c)], LANES - half_x, 1)
                if c == chunks - 1:
                    after = pltpu.roll(strip_out[i], (LANES - half_x - k * STRIP) % LANES, 1)
                else:
                    after = pltpu.roll(out_buf[z, :, lanes(c + 1)], LANES - half_x, 1)
                out_buf[z, :, lanes(c)] = jnp.where(here, v, after)
            return carry

        lax.fori_loop(0, nz // packed, body, 0)

    quotient(0)
    send_shared(1)
    send_free(2)
    back_inner(0)
    blur_edges(1)
    back_outer(0)
    back_x(0)
    stage1(0)
    blur_x_rest((1,))
    stage2(0)
    quotient(1)
    send_shared(2)
    send_free(3)
    back_inner(1)
    stage3(0)
    back_outer(1)
    back_x(1)
    stage1(1)
    blur_x_rest((2, 3))
    stage4(0)
    stage2(1)
    quotient(2)
    send_shared(3)
    back_inner(2)
    stage3(1)
    back_outer(2)
    back_x(2)
    stage1(2)
    stage5(0)
    stage4(1)
    stage2(2)
    quotient(3)
    back_inner(3)
    stage3(2)
    back_outer(3)
    back_x(3)
    stage1(3)
    back_strip()
    stage1(chunks)
    stage5(1)
    realign(0)
    stage4(2)
    stage2(3)
    stage2(chunks)
    stage3(3)
    stage3(chunks)
    stage5(2)
    realign(1)
    stage4(3)
    stage4(chunks)
    stage5(3)
    realign(2)
    stage5(chunks)
    realign(3)

    for c in range(chunks):
        sent = reg.at[c, pl.ds(0, nz - planes)]
        pltpu.make_async_copy(sent, sent, a2a_send.at[c]).wait()

        inner_copy(c).wait_send()
    for c in range(chunks + 1):
        for u in shares(c):
            for d in range(2):
                s1_copy(c, u, d).wait_send()
                s2_copy(c, u, d).wait_send()
    for d in range(2):
        g1_copy(chunks, 0, d).wait_send()
        g2_copy(chunks, 0, d).wait_send()

    @pl.when(has_outer)
    def _():
        for c in range(chunks):
            outer_copy(c).wait_send()
        for n in range(2):
            for h in range(2):
                for d in range(2):
                    pass_copy(n, h, d).wait_send()

    @pl.when(has_left)
    def _():
        for c in range(chunks):
            qh_copy(c, 0).wait_send()

    @pl.when(has_right)
    def _():
        for c in range(chunks):
            qh_copy(c, 1).wait_send()


def solution(mesh):
    nv, nt = mesh.shape["view"], mesh.shape["tile"]

    def on_device(estimate, view_stacks, profile_z, profile_y, profile_x, offsets, coverage):
        nz, ny, nx = estimate.shape
        kz, ky, kx = profile_z.shape[1], profile_y.shape[1], profile_x.shape[1]
        planes = view_stacks.shape[1]
        tx = 4 if nt == 32 else 2
        chunks = nx // LANES
        pad = 8
        half_y = ky // 2
        blk = nz // nv
        sub = blk // UNITS
        strip_planes = nz * STRIP // LANES
        dims = (nv, nt, tx, nz, ny, nx, kz, ky, kx)
        any_spec = pl.BlockSpec(memory_space=pl.ANY)
        smem_spec = pl.BlockSpec(memory_space=pltpu.SMEM)
        dma = pltpu.SemaphoreType.DMA
        return pl.pallas_call(
            functools.partial(rl_kernel, dims),
            out_shape=pltpu.VMEM(estimate.shape, F32),
            in_specs=[any_spec, any_spec] + [smem_spec] * 5,
            out_specs=pl.BlockSpec(memory_space=pltpu.VMEM),
            scratch_shapes=[
                pltpu.VMEM(view_stacks.shape[1:], F32),
                pltpu.VMEM((chunks, nz, ny, LANES), F32),
                pltpu.VMEM((chunks, nz, ny + 2 * pad, LANES), F32),
                pltpu.VMEM((ny + 2 * half_y, nz, nx), F32),
                pltpu.VMEM((ny + 2 * half_y, nz, nx), F32),
                pltpu.VMEM((ny, nz, nx), F32),
                pltpu.VMEM((2, chunks, UNITS, sub // 2, ny, LANES), F32),
                pltpu.VMEM((2, chunks, UNITS, sub, ny, LANES), F32),
                pltpu.VMEM((nz, 2 * LANES), F32),
                pltpu.VMEM((2 * nz, 2 * nz), BF16),
                pltpu.VMEM((2 * nz, 2 * nz), BF16),
                pltpu.VMEM((3 * LANES, 2 * LANES), BF16),
                pltpu.VMEM((2 * LANES, 2 * LANES), BF16),
                pltpu.VMEM((LANES, 2 * LANES), BF16),
                pltpu.VMEM((strip_planes, ny, LANES), F32),
                pltpu.VMEM((strip_planes, ny, LANES), F32),
                pltpu.VMEM((2, strip_planes // nv // 2, ny, LANES), F32),
                pltpu.VMEM((2, strip_planes // nv, ny, LANES), F32),
                dma((planes,)),
                dma((chunks,)),
                dma((chunks,)),
                dma((chunks,)),
                dma((chunks,)),
                dma((chunks,)),
                dma((chunks,)),
                dma((2, 2, 2)),
                dma((2, 2, 2)),
                dma((chunks,)),
                dma((chunks,)),
            ]
            + [dma((chunks, 2))] * 2
            + [dma((chunks + 1, UNITS, 2))] * 8,
            compiler_params=pltpu.CompilerParams(
                collective_id=0, has_side_effects=True, vmem_limit_bytes=60_000_000
            ),
        )(estimate, view_stacks, profile_z, profile_y, profile_x, offsets, coverage)

    return jax.shard_map(
        on_device,
        mesh=mesh,
        in_specs=(
            P(None, "tile", None),
            P("view", "tile", None, None),
            P("view", None),
            P("view", None),
            P("view", None),
            P("view"),
            P("tile", None),
        ),
        out_specs=P(None, "tile", None),
        check_vma=False,
    )
```

```python
import functools

import jax
import jax.numpy as jnp
from jax import lax
from jax.experimental import pallas as pl
from jax.experimental.pallas import tpu as pltpu
from jax.sharding import PartitionSpec as P

MESH = pl.DeviceIdType.MESH
CORES = 2
LANES = 128
UNITS = 2
STRIP = 8
F32 = jnp.float32
BF16 = jnp.bfloat16


def rl_kernel(
    dims,
    est_hbm,
    stack_hbm,
    pz_ref,
    py_ref,
    px_ref,
    off_ref,
    cov_ref,
    out_buf,
    slab,
    reg,
    est_ext,
    zb,
    q_ext,
    part,
    r1,
    r2,
    yq,
    az,
    azt,
    wx,
    wxt,
    wm,
    strip,
    strip_out,
    r1s,
    r2s,
    slab_sem,
    est_load,
    own_sem,
    inner_send,
    inner_recv,
    outer_send,
    outer_recv,
    pass_send,
    pass_recv,
    a2a_send,
    a2a_recv,
    qh_send,
    qh_recv,
    s1_send,
    s1_recv,
    s2_send,
    s2_recv,
    g1_send,
    g1_recv,
    g2_send,
    g2_recv,
):
    nv, nt, tx, nz, ny, nx, kz, ky, kx = dims
    planes = nz // nt
    chunks = nx // LANES
    half_y = ky // 2
    half_z = kz // 2
    half_x = kx // 2
    pad = 8
    tz = nt // (tx * CORES)
    blk = nz // nv
    units = UNITS
    sub = blk // units
    half = sub // 2
    packed = LANES // STRIP
    strip_planes = nz // packed
    strip_blk = strip_planes // nv

    me_v = lax.axis_index("view")
    me_t = lax.axis_index("tile")
    up = lax.rem(me_v + 1, nv)
    down = lax.rem(me_v + nv - 1, nv)
    across = lax.rem(me_v + 2, nv)
    core = lax.rem(me_t, CORES)
    at_x = lax.rem(me_t // CORES, tx)
    at_z = me_t // (CORES * tx)

    def at(v, t):
        return {"view": v, "tile": t}

    def tile_at(dz, dx, dc):
        c = lax.rem(core + dc, CORES)
        x = lax.rem(at_x + dx, tx)
        z = lax.rem(at_z + dz, tz)
        return (z * tx + x) * CORES + c

    def peer(k):
        return tile_at(k // (CORES * tx), lax.rem(k // CORES, tx), lax.rem(k, CORES))

    toward = jnp.where(core == 0, tx - 1, 1)
    away = tx - toward
    half_ring = tx // 2

    def free_peer(i):
        dx = away * lax.rem(i // CORES, 2)
        return tile_at(lax.rem(i // (2 * CORES) + tz // 2, tz), dx, lax.rem(i, CORES))

    def shared_peer(i):
        dx = jnp.where(lax.rem(i // CORES, 2) == 0, half_ring, toward)
        return tile_at(lax.rem(i // (2 * CORES) + tz // 2, tz), dx, lax.rem(i, CORES))

    def lanes(c):
        return pl.ds(c * LANES, LANES)

    def load_slab(p):
        return pltpu.make_async_copy(stack_hbm.at[0, p], slab.at[p], slab_sem.at[p])

    def load_est(c):
        return pltpu.make_async_copy(
            est_hbm.at[:, :, lanes(c)], est_ext.at[c, :, pl.ds(pad, ny), :], est_load.at[c]
        )

    for p in range(planes):
        load_slab(p).start()
    for c in range(chunks):
        load_est(c).start()

    barrier = pltpu.get_barrier_semaphore()

    def greet(k, carry):
        pl.semaphore_signal(barrier, inc=1, device_id=at(me_v, peer(k)), device_id_type=MESH)
        return carry

    lax.fori_loop(1, nt, greet, 0)
    for v in (up, down):
        pl.semaphore_signal(barrier, inc=1, device_id=at(v, me_t), device_id_type=MESH)
    pl.semaphore_wait(barrier, nt - 1 + 2)

    has_left = me_t > 0
    has_right = me_t < nt - 1
    has_outer = jnp.where(core == 0, me_t, nt - 1 - me_t) > 0

    def aligned(row):
        return pl.ds(pl.multiple_of(row, 8), pad)

    def inner_copy(c):
        return pltpu.make_async_remote_copy(
            src_ref=est_hbm.at[:, aligned((1 - core) * (ny - pad)), lanes(c)],
            dst_ref=est_ext.at[c, :, aligned(core * (ny + pad)), :],
            send_sem=inner_send.at[c],
            recv_sem=inner_recv.at[c],
            device_id=at(me_v, me_t + 1 - 2 * core),
            device_id_type=MESH,
        )

    def outer_copy(c):
        share = pl.ds(me_v * blk, blk)
        return pltpu.make_async_remote_copy(
            src_ref=est_hbm.at[share, aligned(core * (ny - pad)), lanes(c)],
            dst_ref=est_ext.at[c, share, aligned((1 - core) * (ny + pad)), :],
            send_sem=outer_send.at[c],
            recv_sem=outer_recv.at[c],
            device_id=at(me_v, lax.rem(me_t + nt - 1 + 2 * core, nt)),
            device_id_type=MESH,
        )

    outer_rows = aligned(core * (ny + pad))

    def pass_copy(n, h, d):
        if n == 0:
            share = pl.ds(me_v * blk, blk)
        else:
            share = pl.ds((down if d == 0 else up) * blk + d * (blk // 2), blk // 2)
        region = est_ext.at[pl.ds(h * (chunks // 2), chunks // 2), share, outer_rows, :]
        return pltpu.make_async_remote_copy(
            src_ref=region,
            dst_ref=region,
            send_sem=pass_send.at[n, h, d],
            recv_sem=pass_recv.at[n, h, d],
            device_id=at(up if d == 0 else down, me_t),
            device_id_type=MESH,
        )

    @pl.when(has_outer)
    def _():
        for c in range(chunks):
            outer_copy(c).start()

    for c in range(chunks):
        inner_copy(c).start()

    off = off_ref[0]
    turn = lax.rem(LANES - off, LANES)
    rows_block = 64
    lane = lax.broadcasted_iota(jnp.int32, (rows_block, LANES), 1) + off
    over = lane >= LANES
    under = lane < 0
    nothing = jnp.zeros((rows_block, LANES), F32)

    for p in range(planes):
        load_slab(p).wait()

        def shift(i, carry, p=p):
            r = pl.ds(pl.multiple_of(i * rows_block, rows_block), rows_block)
            v = [nothing] + [pltpu.roll(slab[p, r, lanes(c)], turn, 1) for c in range(chunks)] + [nothing]
            for c in range(chunks):
                slab[p, r, lanes(c)] = jnp.where(over, v[c + 2], jnp.where(under, v[c], v[c + 1]))
            return carry

        lax.fori_loop(0, slab.shape[1] // rows_block, shift, 0)

    my_planes = pl.ds(me_t * planes, planes)

    def a2a_copy(c, t):
        return pltpu.make_async_remote_copy(
            src_ref=slab.at[:, pl.ds(pl.multiple_of(t * ny, 8), ny), lanes(c)],
            dst_ref=reg.at[c, my_planes],
            send_sem=a2a_send.at[c],
            recv_sem=a2a_recv.at[c],
            device_id=at(me_v, t),
            device_id_type=MESH,
        )

    def send_free(c):
        def send(i, carry):
            a2a_copy(c, free_peer(i)).start()
            return carry

        own = tz // 2 * 2 * CORES
        lax.fori_loop(0, own, send, 0)
        lax.fori_loop(own + 1, nt // 2, send, 0)

    def send_shared(c):
        def send(i, carry):
            a2a_copy(c, shared_peer(i)).start()
            return carry

        lax.fori_loop(0, nt // 2, send, 0)

    send_shared(0)
    send_free(0)
    send_free(1)

    def own_planes(c):
        mine = slab.at[:, pl.ds(pl.multiple_of(me_t * ny, 8), ny), lanes(c)]
        return pltpu.make_async_copy(mine, reg.at[c, my_planes], own_sem.at[c])

    for c in range(chunks):
        own_planes(c).start()

    def pass_on(n, h):
        @pl.when(has_outer)
        def _():
            if n == 0:
                for c in range(h * chunks // 2, (h + 1) * chunks // 2):
                    outer_copy(c).wait_recv()
            for d in range(2):
                if n > 0:
                    pass_copy(n - 1, h, d).wait_recv()
                if n < 2:
                    pass_copy(n, h, d).start()

    pass_on(0, 0)
    pass_on(0, 1)

    def total(ref, count):
        return lax.fori_loop(1, count, lambda a, s: s + ref[0, a], ref[0, 0])

    def bands(ref, count, gap, scale):
        zero = jnp.zeros(gap.shape, F32)
        full = lax.fori_loop(0, count, lambda a, m: m + jnp.where(gap == a, ref[0, a], 0.0), zero)
        full = full / scale
        hi = full.astype(BF16)
        lo = (full - hi.astype(F32)).astype(BF16)
        return hi, lo

    scale_zy = jnp.full((nz, nz), total(pz_ref, kz), F32) * jnp.full((nz, nz), total(py_ref, ky), F32)
    row = lax.broadcasted_iota(jnp.int32, (nz, nz), 0)
    col = lax.broadcasted_iota(jnp.int32, (nz, nz), 1)
    for ref, gap in ((az, col - row + half_z), (azt, row - col + half_z)):
        hi, lo = bands(pz_ref, kz, gap, scale_zy)
        ref[...] = jnp.concatenate(
            [jnp.concatenate([hi, hi], axis=1), jnp.concatenate([lo, lo], axis=1)], axis=0
        )
    for ref, taps in ((wx, kx), (wxt, kx), (wm, kx)):
        shape = (ref.shape[0], LANES)
        row = lax.broadcasted_iota(jnp.int32, shape, 0)
        col = lax.broadcasted_iota(jnp.int32, shape, 1)
        if ref is wx:
            gap = row - col - LANES + half_x
        elif ref is wxt:
            gap = col - row + LANES
        else:
            gap = lax.rem(col, STRIP) - row + LANES
        hi, lo = bands(px_ref, taps, gap, jnp.full(shape, total(px_ref, kx), F32))
        ref[...] = jnp.concatenate([hi, lo], axis=1)

    def split(v):
        hi = v.astype(BF16)
        return hi, (v - hi.astype(F32)).astype(BF16)

    def z_pass(matrix, v):
        hi, lo = split(v)
        r = jnp.dot(matrix[...], jnp.concatenate([hi, lo], axis=0), preferred_element_type=F32)
        return r[:nz] + r[nz:]

    def x_pass(matrix, src, y0, count, c, reach):
        first, last = max(c - 1, 0), min(c + reach, chunks - 1)
        v = src[pl.ds(y0, count), :, first * LANES : (last + 1) * LANES]
        v = v.reshape(count * nz, v.shape[2])
        hi, lo = split(v)
        w = matrix[(first - c + 1) * LANES : (last - c + 2) * LANES, :]
        r = jnp.dot(
            jnp.concatenate([hi, lo], axis=1),
            jnp.concatenate([w, w], axis=0),
            preferred_element_type=F32,
        )
        return r[:, :LANES] + r[:, LANES:]

    rows_ext = ny + 2 * pad
    est_rows = est_ext.reshape(chunks, nz * rows_ext, LANES)
    first_row = pad - half_y

    def blur_z(h):
        cs = range(h * chunks // 2, (h + 1) * chunks // 2)
        into = pl.ds(h * nx // 2, nx // 2)

        def body(i, carry):
            rows = pl.ds(i + first_row, nz, stride=rows_ext)
            zb[i, :, into] = z_pass(az, jnp.concatenate([est_rows[c, rows, :] for c in cs], axis=1))
            return carry

        return body

    zblock = min(64, nz)

    def blur_y(h):
        into = pl.ds(h * nx // 2, nx // 2)

        def body(y, carry):
            def inner(j, carry):
                zs = pl.ds(pl.multiple_of(j * zblock, zblock), zblock)
                acc = py_ref[0, 0] * zb[y, zs, into]
                for b in range(1, ky):
                    acc = acc + py_ref[0, b] * zb[y + b, zs, into]
                part[y, zs, into] = acc
                return carry

            return lax.fori_loop(0, nz // zblock, inner, carry)

        return body

    ygroup = 4

    def blur_x(cs):
        def body(i, carry):
            y0 = i * ygroup
            for c in cs:
                r = x_pass(wx, part, y0, ygroup, c, 1)
                q_ext[pl.ds(half_y + y0, ygroup), :, lanes(c)] = r.reshape(ygroup, nz, LANES)
            return carry

        return body


    @pl.when(jnp.logical_not(has_outer))
    def _():
        def body(i, carry):
            for c in range(chunks):
                est_ext[c, i, outer_rows, :] = jnp.zeros((pad, LANES), F32)
            return carry

        lax.fori_loop(0, nz, body, 0)

    for c in range(chunks):
        load_est(c).wait()
    def blur_own(h):
        lax.fori_loop(half_y, half_y + ny, blur_z(h), 0)
        if h == 0:
            pass_on(1, h)
        lax.fori_loop(pad, ny - pad, blur_y(h), 0)

    blur_own(0)
    lax.fori_loop(pad // ygroup, (ny - pad) // ygroup, blur_x((0,)), 0)
    pass_on(1, 1)

    def side_start(inner, last):
        return jnp.where((core == 0) == inner, last, 0)

    def from_row(body, first):
        return lambda i, carry: body(first + i, carry)

    def blur_edge(h, inner):
        if inner:
            for c in range(h * chunks // 2, (h + 1) * chunks // 2):
                inner_copy(c).wait_recv()
        else:
            pass_on(2, h)
        lax.fori_loop(0, half_y, from_row(blur_z(h), side_start(inner, half_y + ny)), 0)
        lax.fori_loop(0, pad, from_row(blur_y(h), side_start(inner, ny - pad)), 0)

    def blur_x_edge(cs, inner):
        first = side_start(inner, (ny - pad) // ygroup)
        lax.fori_loop(0, pad // ygroup, from_row(blur_x(cs), first), 0)

    blur_edge(0, True)
    blur_x_edge((0,), True)
    blur_edge(0, False)
    blur_x_edge((0,), False)

    halo = jnp.zeros((half_y, nz, nx), F32)

    @pl.when(jnp.logical_not(has_left))
    def _():
        q_ext[pl.ds(0, half_y)] = halo

    @pl.when(jnp.logical_not(has_right))
    def _():
        q_ext[pl.ds(half_y + ny, half_y)] = halo

    cov = jnp.full((nz, LANES), cov_ref[0, me_v].astype(F32), F32)
    count = cov_ref[0, 0]
    for v in range(1, nv):
        count = count + cov_ref[0, v]
    count = jnp.full((ny, LANES), count.astype(F32), F32)

    for c in range(chunks):
        own_planes(c).wait()
    reg_rows = reg.reshape(chunks, nz * ny, LANES)

    def qh_copy(c, side):
        target = me_t - 1 if side == 0 else me_t + 1
        rows = pl.ds(half_y, half_y) if side == 0 else pl.ds(ny, half_y)
        into = pl.ds(half_y + ny, half_y) if side == 0 else pl.ds(0, half_y)
        return pltpu.make_async_remote_copy(
            src_ref=q_ext.at[rows, :, lanes(c)],
            dst_ref=q_ext.at[into, :, lanes(c)],
            send_sem=qh_send.at[c, side],
            recv_sem=qh_recv.at[c, side],
            device_id=at(me_v, lax.rem(target + nt, nt)),
            device_id_type=MESH,
        )

    def quotient(c):
        arrived = reg.at[c, pl.ds(0, nz - planes)]
        pltpu.make_async_copy(arrived, arrived, a2a_recv.at[c]).wait()

        def body(y, carry):
            v = reg_rows[c, pl.ds(y, nz, stride=ny), :]
            q_ext[half_y + y, :, lanes(c)] = v / q_ext[half_y + y, :, lanes(c)]
            return carry

        lax.fori_loop(0, ny, body, 0)

        @pl.when(has_left)
        def _():
            qh_copy(c, 0).start()

        @pl.when(has_right)
        def _():
            qh_copy(c, 1).start()

    def back_rows(c, first, count):
        def body(i, carry):
            r = x_pass(wxt, zb, i * ygroup, ygroup, c, 0).reshape(ygroup, nz, LANES)
            for k in range(ygroup):
                reg_rows[c, pl.ds(i * ygroup + k, nz, stride=ny), :] = cov * r[k]
            return carry

        lax.fori_loop(0, count // ygroup, from_row(body, first // ygroup), 0)

    def back_pairs(c, first, count):
        def body(i, carry):
            for k in range(2):
                acc = py_ref[0, ky - 1] * q_ext[2 * i + k, :, lanes(c)]
                for b in range(1, ky):
                    acc = acc + py_ref[0, ky - 1 - b] * q_ext[2 * i + k + b, :, lanes(c)]
                yq[:, k * LANES : (k + 1) * LANES] = acc
            r = z_pass(azt, yq[...])
            for k in range(2):
                zb[2 * i + k, :, lanes(c)] = r[:, k * LANES : (k + 1) * LANES]
            return carry

        lax.fori_loop(0, count // 2, from_row(body, first // 2), 0)

    def back_inner(c):
        back_pairs(c, pad, ny - 2 * pad)

        @pl.when(core == 0)
        def _():
            qh_copy(c, 0).wait_recv()

        @pl.when(core == 1)
        def _():
            qh_copy(c, 1).wait_recv()

        first = side_start(True, ny - pad)
        back_pairs(c, first, pad)
        back_rows(c, pad, ny - 2 * pad)
        back_rows(c, first, pad)

    def back_outer(c):
        @pl.when(jnp.logical_and(core == 0, has_left))
        def _():
            qh_copy(c, 1).wait_recv()

        @pl.when(jnp.logical_and(core == 1, has_right))
        def _():
            qh_copy(c, 0).wait_recv()

        first = side_start(False, ny - pad)
        back_pairs(c, first, pad)
        back_rows(c, first, pad)

    sums = reg
    strip_rows = strip.reshape(strip_planes * ny, LANES)
    row = lax.broadcasted_iota(jnp.int32, (nz, LANES), 0)
    col = lax.broadcasted_iota(jnp.int32, (nz, LANES), 1)
    in_strip = lax.rem(row, packed) == col // STRIP

    def back_strip():
        def body(i, carry):
            r = x_pass(wm, zb, i * ygroup, ygroup, chunks, 0).reshape(ygroup, nz, LANES)
            for k in range(ygroup):
                v = jnp.where(in_strip, cov * r[k], 0.0)
                v = jnp.sum(v.reshape(strip_planes, packed, LANES), axis=1)
                strip_rows[pl.ds(i * ygroup + k, strip_planes, stride=ny), :] = v
            return carry

        lax.fori_loop(0, ny // ygroup, body, 0)

    def copy_to(src, dst, send, recv, c, u, d):
        return pltpu.make_async_remote_copy(
            src_ref=src,
            dst_ref=dst,
            send_sem=send.at[c, u, d],
            recv_sem=recv.at[c, u, d],
            device_id=at(up if d == 0 else down, me_t),
            device_id_type=MESH,
        )

    def shares(c):
        return range(1) if c == chunks else range(units)

    def s1_copy(c, u, d):
        if c == chunks:
            src, dst = strip.at[pl.ds(across * strip_blk + d * (strip_blk // 2), strip_blk // 2)], r1s.at[d]
        else:
            start = across * blk + u * sub + (0 if d == 0 else half)
            src, dst = sums.at[c, pl.ds(start, half)], r1.at[d, c, u]
        return copy_to(src, dst, s1_send, s1_recv, c, u, d)

    def s2_copy(c, u, d):
        owner = up if d == 0 else down
        if c == chunks:
            src, dst = strip.at[pl.ds(owner * strip_blk, strip_blk)], r2s.at[d]
        else:
            src, dst = sums.at[c, pl.ds(owner * blk + u * sub, sub)], r2.at[d, c, u]
        return copy_to(src, dst, s2_send, s2_recv, c, u, d)

    def g1_copy(c, u, d):
        if c == chunks:
            mine = strip_out.at[pl.ds(me_v * strip_blk, strip_blk)]
        else:
            mine = out_buf.at[pl.ds(me_v * blk + u * sub, sub), :, lanes(c)]
        return copy_to(mine, mine, g1_send, g1_recv, c, u, d)

    def g2_copy(c, u, d):
        owner = down if d == 0 else up
        if c == chunks:
            piece = strip_out.at[pl.ds(owner * strip_blk + d * (strip_blk // 2), strip_blk // 2)]
        else:
            start = owner * blk + u * sub + (0 if d == 0 else half)
            piece = out_buf.at[pl.ds(start, half), :, lanes(c)]
        return copy_to(piece, piece, g2_send, g2_recv, c, u, d)

    def stage1(c):
        for u in shares(c):
            for d in range(2):
                s1_copy(c, u, d).start()

    def stage2(c):
        for u in shares(c):
            for d in range(2):
                s1_copy(c, u, d).wait_recv()
                owner = up if d == 0 else down
                if c == chunks:
                    at_plane = pl.ds(owner * strip_blk + d * (strip_blk // 2), strip_blk // 2)
                    strip[at_plane] = strip[at_plane] + r1s[d]
                else:
                    start = owner * blk + u * sub + (0 if d == 0 else half)

                    def body(i, carry, u=u, d=d, start=start):
                        sums[c, start + i] = sums[c, start + i] + r1[d, c, u, i]
                        return carry

                    lax.fori_loop(0, half, body, 0)
                s2_copy(c, u, d).start()

    lane_row = lax.broadcasted_iota(jnp.int32, (ny, LANES), 1)
    own_rows = pl.ds(pad, ny)

    def stage3(c):
        for u in shares(c):
            for d in range(2):
                s2_copy(c, u, d).wait_recv()
            if c == chunks:

                def body(i, carry):
                    z = me_v * strip_blk + i
                    est = jnp.zeros((ny, LANES), F32)
                    for k in range(packed):
                        v = est_ext[chunks - 1, z * packed + k, own_rows, :]
                        v = pltpu.roll(v, (k * STRIP + half_x) % LANES, 1)
                        est = jnp.where(lane_row // STRIP == k, v, est)
                    merged = strip[z] + (r2s[0, i] + r2s[1, i])
                    strip_out[z] = est * merged / count
                    return carry

                lax.fori_loop(0, strip_blk, body, 0)
            else:

                def body(i, carry, u=u):
                    z = me_v * blk + u * sub + i
                    merged = sums[c, z] + (r2[0, c, u, i] + r2[1, c, u, i])
                    est = pltpu.roll(est_ext[c, z, own_rows, :], half_x, 1)
                    if c > 0:
                        before = pltpu.roll(est_ext[c - 1, z, own_rows, :], half_x, 1)
                        est = jnp.where(lane_row < half_x, before, est)
                    out_buf[z, :, lanes(c)] = est * merged / count
                    return carry

                lax.fori_loop(0, sub, body, 0)
            for d in range(2):
                g1_copy(c, u, d).start()

    def stage4(c):
        for u in shares(c):
            for d in range(2):
                g1_copy(c, u, d).wait_recv()
                g2_copy(c, u, d).start()

    def stage5(c):
        for u in shares(c):
            for d in range(2):
                g2_copy(c, u, d).wait_recv()

    def realign(c):
        for u in shares(c):
            for d in range(2):
                g1_copy(c, u, d).wait_send()
                g2_copy(c, u, d).wait_send()
        here = lane_row < LANES - half_x

        def body(i, carry):
            for k in range(packed):
                z = i * packed + k
                v = pltpu.roll(out_buf[z, :, lanes(c)], LANES - half_x, 1)
                if c == chunks - 1:
                    after = pltpu.roll(strip_out[i], (LANES - half_x - k * STRIP) % LANES, 1)
                else:
                    after = pltpu.roll(out_buf[z, :, lanes(c + 1)], LANES - half_x, 1)
                out_buf[z, :, lanes(c)] = jnp.where(here, v, after)
            return carry

        lax.fori_loop(0, nz // packed, body, 0)

    quotient(0)
    send_shared(1)
    back_inner(0)
    blur_own(1)
    blur_edge(1, True)
    back_outer(0)
    stage1(0)
    blur_edge(1, False)
    lax.fori_loop(0, ny // ygroup, blur_x((1,)), 0)
    stage2(0)
    quotient(1)
    send_shared(2)
    send_free(2)
    back_inner(1)
    stage3(0)
    back_outer(1)
    stage1(1)
    lax.fori_loop(0, ny // ygroup, blur_x((2, 3)), 0)
    stage4(0)
    stage2(1)
    quotient(2)
    send_shared(3)
    send_free(3)
    back_inner(2)
    stage3(1)
    back_outer(2)
    stage1(2)
    stage5(0)
    stage4(1)
    quotient(3)
    stage2(2)
    back_inner(3)
    back_outer(3)
    stage1(3)
    stage3(2)
    back_strip()
    stage1(chunks)
    stage5(1)
    realign(0)
    stage2(3)
    stage2(chunks)
    stage4(2)
    stage3(3)
    stage3(chunks)
    stage5(2)
    realign(1)
    stage4(3)
    stage4(chunks)
    stage5(3)
    realign(2)
    stage5(chunks)
    realign(3)

    for c in range(chunks):
        sent = reg.at[c, pl.ds(0, nz - planes)]
        pltpu.make_async_copy(sent, sent, a2a_send.at[c]).wait()

        inner_copy(c).wait_send()
    for c in range(chunks + 1):
        for u in shares(c):
            for d in range(2):
                s1_copy(c, u, d).wait_send()
                s2_copy(c, u, d).wait_send()
    for d in range(2):
        g1_copy(chunks, 0, d).wait_send()
        g2_copy(chunks, 0, d).wait_send()

    @pl.when(has_outer)
    def _():
        for c in range(chunks):
            outer_copy(c).wait_send()
        for n in range(2):
            for h in range(2):
                for d in range(2):
                    pass_copy(n, h, d).wait_send()

    @pl.when(has_left)
    def _():
        for c in range(chunks):
            qh_copy(c, 0).wait_send()

    @pl.when(has_right)
    def _():
        for c in range(chunks):
            qh_copy(c, 1).wait_send()


def solution(mesh):
    nv, nt = mesh.shape["view"], mesh.shape["tile"]

    def on_device(estimate, view_stacks, profile_z, profile_y, profile_x, offsets, coverage):
        nz, ny, nx = estimate.shape
        kz, ky, kx = profile_z.shape[1], profile_y.shape[1], profile_x.shape[1]
        planes = view_stacks.shape[1]
        tx = 4 if nt == 32 else 2
        chunks = nx // LANES
        pad = 8
        half_y = ky // 2
        blk = nz // nv
        sub = blk // UNITS
        strip_planes = nz * STRIP // LANES
        dims = (nv, nt, tx, nz, ny, nx, kz, ky, kx)
        any_spec = pl.BlockSpec(memory_space=pl.ANY)
        smem_spec = pl.BlockSpec(memory_space=pltpu.SMEM)
        dma = pltpu.SemaphoreType.DMA
        return pl.pallas_call(
            functools.partial(rl_kernel, dims),
            out_shape=pltpu.VMEM(estimate.shape, F32),
            in_specs=[any_spec, any_spec] + [smem_spec] * 5,
            out_specs=pl.BlockSpec(memory_space=pltpu.VMEM),
            scratch_shapes=[
                pltpu.VMEM(view_stacks.shape[1:], F32),
                pltpu.VMEM((chunks, nz, ny, LANES), F32),
                pltpu.VMEM((chunks, nz, ny + 2 * pad, LANES), F32),
                pltpu.VMEM((ny + 2 * half_y, nz, nx), F32),
                pltpu.VMEM((ny + 2 * half_y, nz, nx), F32),
                pltpu.VMEM((ny, nz, nx), F32),
                pltpu.VMEM((2, chunks, UNITS, sub // 2, ny, LANES), F32),
                pltpu.VMEM((2, chunks, UNITS, sub, ny, LANES), F32),
                pltpu.VMEM((nz, 2 * LANES), F32),
                pltpu.VMEM((2 * nz, 2 * nz), BF16),
                pltpu.VMEM((2 * nz, 2 * nz), BF16),
                pltpu.VMEM((3 * LANES, 2 * LANES), BF16),
                pltpu.VMEM((2 * LANES, 2 * LANES), BF16),
                pltpu.VMEM((LANES, 2 * LANES), BF16),
                pltpu.VMEM((strip_planes, ny, LANES), F32),
                pltpu.VMEM((strip_planes, ny, LANES), F32),
                pltpu.VMEM((2, strip_planes // nv // 2, ny, LANES), F32),
                pltpu.VMEM((2, strip_planes // nv, ny, LANES), F32),
                dma((planes,)),
                dma((chunks,)),
                dma((chunks,)),
                dma((chunks,)),
                dma((chunks,)),
                dma((chunks,)),
                dma((chunks,)),
                dma((2, 2, 2)),
                dma((2, 2, 2)),
                dma((chunks,)),
                dma((chunks,)),
            ]
            + [dma((chunks, 2))] * 2
            + [dma((chunks + 1, UNITS, 2))] * 8,
            compiler_params=pltpu.CompilerParams(
                collective_id=0, has_side_effects=True, vmem_limit_bytes=60_000_000
            ),
        )(estimate, view_stacks, profile_z, profile_y, profile_x, offsets, coverage)

    return jax.shard_map(
        on_device,
        mesh=mesh,
        in_specs=(
            P(None, "tile", None),
            P("view", "tile", None, None),
            P("view", None),
            P("view", None),
            P("view", None),
            P("view"),
            P("tile", None),
        ),
        out_specs=P(None, "tile", None),
        check_vma=False,
    )
```

```python
import functools

import jax
import jax.numpy as jnp
from jax import lax
from jax.experimental import pallas as pl
from jax.experimental.pallas import tpu as pltpu
from jax.sharding import PartitionSpec as P

MESH = pl.DeviceIdType.MESH
CORES = 2
LANES = 128
UNITS = 2
STRIP = 8
F32 = jnp.float32
BF16 = jnp.bfloat16


def rl_kernel(
    dims,
    est_hbm,
    stack_hbm,
    pz_ref,
    py_ref,
    px_ref,
    off_ref,
    cov_ref,
    out_buf,
    slab,
    reg,
    est_ext,
    zb,
    q_ext,
    part,
    r1,
    r2,
    yq,
    az,
    azt,
    wx,
    wxt,
    wm,
    strip,
    strip_out,
    r1s,
    r2s,
    slab_sem,
    est_load,
    own_sem,
    inner_send,
    inner_recv,
    outer_send,
    outer_recv,
    pass_send,
    pass_recv,
    a2a_send,
    a2a_recv,
    qh_send,
    qh_recv,
    s1_send,
    s1_recv,
    s2_send,
    s2_recv,
    g1_send,
    g1_recv,
    g2_send,
    g2_recv,
):
    nv, nt, tx, nz, ny, nx, kz, ky, kx = dims
    planes = nz // nt
    chunks = nx // LANES
    half_y = ky // 2
    half_z = kz // 2
    half_x = kx // 2
    pad = 8
    tz = nt // (tx * CORES)
    blk = nz // nv
    units = UNITS
    sub = blk // units
    half = sub // 2
    packed = LANES // STRIP
    strip_planes = nz // packed
    strip_blk = strip_planes // nv

    me_v = lax.axis_index("view")
    me_t = lax.axis_index("tile")
    up = lax.rem(me_v + 1, nv)
    down = lax.rem(me_v + nv - 1, nv)
    across = lax.rem(me_v + 2, nv)
    core = lax.rem(me_t, CORES)
    at_x = lax.rem(me_t // CORES, tx)
    at_z = me_t // (CORES * tx)

    def at(v, t):
        return {"view": v, "tile": t}

    def tile_at(dz, dx, dc):
        c = lax.rem(core + dc, CORES)
        x = lax.rem(at_x + dx, tx)
        z = lax.rem(at_z + dz, tz)
        return (z * tx + x) * CORES + c

    def peer(k):
        return tile_at(k // (CORES * tx), lax.rem(k // CORES, tx), lax.rem(k, CORES))

    toward = jnp.where(core == 0, tx - 1, 1)
    away = tx - toward
    half_ring = tx // 2

    def free_peer(i):
        dx = away * lax.rem(i // CORES, 2)
        return tile_at(lax.rem(i // (2 * CORES) + tz // 2, tz), dx, lax.rem(i, CORES))

    def shared_peer(i):
        dx = jnp.where(lax.rem(i // CORES, 2) == 0, half_ring, toward)
        return tile_at(lax.rem(i // (2 * CORES) + tz // 2, tz), dx, lax.rem(i, CORES))

    def lanes(c):
        return pl.ds(c * LANES, LANES)

    def load_slab(p):
        return pltpu.make_async_copy(stack_hbm.at[0, p], slab.at[p], slab_sem.at[p])

    def load_est(c):
        return pltpu.make_async_copy(
            est_hbm.at[:, :, lanes(c)], est_ext.at[c, :, pl.ds(pad, ny), :], est_load.at[c]
        )

    for p in range(planes):
        load_slab(p).start()
    for c in range(chunks):
        load_est(c).start()

    barrier = pltpu.get_barrier_semaphore()

    def greet(k, carry):
        pl.semaphore_signal(barrier, inc=1, device_id=at(me_v, peer(k)), device_id_type=MESH)
        return carry

    lax.fori_loop(1, nt, greet, 0)
    for v in (up, down):
        pl.semaphore_signal(barrier, inc=1, device_id=at(v, me_t), device_id_type=MESH)
    pl.semaphore_wait(barrier, nt - 1 + 2)

    has_left = me_t > 0
    has_right = me_t < nt - 1
    has_outer = jnp.where(core == 0, me_t, nt - 1 - me_t) > 0

    def aligned(row):
        return pl.ds(pl.multiple_of(row, 8), pad)

    def inner_copy(c):
        return pltpu.make_async_remote_copy(
            src_ref=est_hbm.at[:, aligned((1 - core) * (ny - pad)), lanes(c)],
            dst_ref=est_ext.at[c, :, aligned(core * (ny + pad)), :],
            send_sem=inner_send.at[c],
            recv_sem=inner_recv.at[c],
            device_id=at(me_v, me_t + 1 - 2 * core),
            device_id_type=MESH,
        )

    def outer_copy(c):
        share = pl.ds(me_v * blk, blk)
        return pltpu.make_async_remote_copy(
            src_ref=est_hbm.at[share, aligned(core * (ny - pad)), lanes(c)],
            dst_ref=est_ext.at[c, share, aligned((1 - core) * (ny + pad)), :],
            send_sem=outer_send.at[c],
            recv_sem=outer_recv.at[c],
            device_id=at(me_v, lax.rem(me_t + nt - 1 + 2 * core, nt)),
            device_id_type=MESH,
        )

    outer_rows = aligned(core * (ny + pad))

    def pass_copy(n, h, d):
        if n == 0:
            share = pl.ds(me_v * blk, blk)
        else:
            share = pl.ds((down if d == 0 else up) * blk + d * (blk // 2), blk // 2)
        region = est_ext.at[pl.ds(h * (chunks // 2), chunks // 2), share, outer_rows, :]
        return pltpu.make_async_remote_copy(
            src_ref=region,
            dst_ref=region,
            send_sem=pass_send.at[n, h, d],
            recv_sem=pass_recv.at[n, h, d],
            device_id=at(up if d == 0 else down, me_t),
            device_id_type=MESH,
        )

    @pl.when(has_outer)
    def _():
        for c in range(chunks):
            outer_copy(c).start()

    for c in range(chunks):
        inner_copy(c).start()

    off = off_ref[0]
    turn = lax.rem(LANES - off, LANES)
    rows_block = 64
    lane = lax.broadcasted_iota(jnp.int32, (rows_block, LANES), 1) + off
    over = lane >= LANES
    under = lane < 0
    nothing = jnp.zeros((rows_block, LANES), F32)

    for p in range(planes):
        load_slab(p).wait()

        def shift(i, carry, p=p):
            r = pl.ds(pl.multiple_of(i * rows_block, rows_block), rows_block)
            v = [nothing] + [pltpu.roll(slab[p, r, lanes(c)], turn, 1) for c in range(chunks)] + [nothing]
            for c in range(chunks):
                slab[p, r, lanes(c)] = jnp.where(over, v[c + 2], jnp.where(under, v[c], v[c + 1]))
            return carry

        lax.fori_loop(0, slab.shape[1] // rows_block, shift, 0)

    my_planes = pl.ds(me_t * planes, planes)

    def a2a_copy(c, t):
        return pltpu.make_async_remote_copy(
            src_ref=slab.at[:, pl.ds(pl.multiple_of(t * ny, 8), ny), lanes(c)],
            dst_ref=reg.at[c, my_planes],
            send_sem=a2a_send.at[c],
            recv_sem=a2a_recv.at[c],
            device_id=at(me_v, t),
            device_id_type=MESH,
        )

    def send_free(c):
        def send(i, carry):
            a2a_copy(c, free_peer(i)).start()
            return carry

        own = tz // 2 * 2 * CORES
        lax.fori_loop(0, own, send, 0)
        lax.fori_loop(own + 1, nt // 2, send, 0)

    def send_shared(c):
        def send(i, carry):
            a2a_copy(c, shared_peer(i)).start()
            return carry

        lax.fori_loop(0, nt // 2, send, 0)

    send_shared(0)
    send_free(0)
    send_free(1)

    def own_planes(c):
        mine = slab.at[:, pl.ds(pl.multiple_of(me_t * ny, 8), ny), lanes(c)]
        return pltpu.make_async_copy(mine, reg.at[c, my_planes], own_sem.at[c])

    for c in range(chunks):
        own_planes(c).start()

    def pass_on(n, h):
        @pl.when(has_outer)
        def _():
            if n == 0:
                for c in range(h * chunks // 2, (h + 1) * chunks // 2):
                    outer_copy(c).wait_recv()
            for d in range(2):
                if n > 0:
                    pass_copy(n - 1, h, d).wait_recv()
                if n < 2:
                    pass_copy(n, h, d).start()

    pass_on(0, 0)
    pass_on(0, 1)

    def total(ref, count):
        return lax.fori_loop(1, count, lambda a, s: s + ref[0, a], ref[0, 0])

    def bands(ref, count, gap, scale):
        zero = jnp.zeros(gap.shape, F32)
        full = lax.fori_loop(0, count, lambda a, m: m + jnp.where(gap == a, ref[0, a], 0.0), zero)
        full = full / scale
        hi = full.astype(BF16)
        lo = (full - hi.astype(F32)).astype(BF16)
        return hi, lo

    scale_zy = jnp.full((nz, nz), total(pz_ref, kz), F32) * jnp.full((nz, nz), total(py_ref, ky), F32)
    row = lax.broadcasted_iota(jnp.int32, (nz, nz), 0)
    col = lax.broadcasted_iota(jnp.int32, (nz, nz), 1)
    for ref, gap in ((az, col - row + half_z), (azt, row - col + half_z)):
        hi, lo = bands(pz_ref, kz, gap, scale_zy)
        ref[...] = jnp.concatenate(
            [jnp.concatenate([hi, hi], axis=1), jnp.concatenate([lo, lo], axis=1)], axis=0
        )
    for ref, taps in ((wx, kx), (wxt, kx), (wm, kx)):
        shape = (ref.shape[0], LANES)
        row = lax.broadcasted_iota(jnp.int32, shape, 0)
        col = lax.broadcasted_iota(jnp.int32, shape, 1)
        if ref is wx:
            gap = row - col - LANES + half_x
        elif ref is wxt:
            gap = col - row + LANES
        else:
            gap = lax.rem(col, STRIP) - row + LANES
        hi, lo = bands(px_ref, taps, gap, jnp.full(shape, total(px_ref, kx), F32))
        ref[...] = jnp.concatenate([hi, lo], axis=1)

    def split(v):
        hi = v.astype(BF16)
        return hi, (v - hi.astype(F32)).astype(BF16)

    def z_pass(matrix, v):
        hi, lo = split(v)
        r = jnp.dot(matrix[...], jnp.concatenate([hi, lo], axis=0), preferred_element_type=F32)
        return r[:nz] + r[nz:]

    def x_pass(matrix, src, y0, count, c, reach):
        first, last = max(c - 1, 0), min(c + reach, chunks - 1)
        v = src[pl.ds(y0, count), :, first * LANES : (last + 1) * LANES]
        v = v.reshape(count * nz, v.shape[2])
        hi, lo = split(v)
        w = matrix[(first - c + 1) * LANES : (last - c + 2) * LANES, :]
        r = jnp.dot(
            jnp.concatenate([hi, lo], axis=1),
            jnp.concatenate([w, w], axis=0),
            preferred_element_type=F32,
        )
        return r[:, :LANES] + r[:, LANES:]

    rows_ext = ny + 2 * pad
    est_rows = est_ext.reshape(chunks, nz * rows_ext, LANES)
    first_row = pad - half_y

    def blur_z(h):
        cs = range(h * chunks // 2, (h + 1) * chunks // 2)
        into = pl.ds(h * nx // 2, nx // 2)

        def body(i, carry):
            rows = pl.ds(i + first_row, nz, stride=rows_ext)
            zb[i, :, into] = z_pass(az, jnp.concatenate([est_rows[c, rows, :] for c in cs], axis=1))
            return carry

        return body

    zblock = min(64, nz)

    def blur_y(h):
        into = pl.ds(h * nx // 2, nx // 2)

        def body(y, carry):
            def inner(j, carry):
                zs = pl.ds(pl.multiple_of(j * zblock, zblock), zblock)
                acc = py_ref[0, 0] * zb[y, zs, into]
                for b in range(1, ky):
                    acc = acc + py_ref[0, b] * zb[y + b, zs, into]
                part[y, zs, into] = acc
                return carry

            return lax.fori_loop(0, nz // zblock, inner, carry)

        return body

    ygroup = 4

    def blur_x(cs):
        def body(i, carry):
            y0 = i * ygroup
            for c in cs:
                r = x_pass(wx, part, y0, ygroup, c, 1)
                q_ext[pl.ds(half_y + y0, ygroup), :, lanes(c)] = r.reshape(ygroup, nz, LANES)
            return carry

        return body


    @pl.when(jnp.logical_not(has_outer))
    def _():
        def body(i, carry):
            for c in range(chunks):
                est_ext[c, i, outer_rows, :] = jnp.zeros((pad, LANES), F32)
            return carry

        lax.fori_loop(0, nz, body, 0)

    for c in range(chunks):
        load_est(c).wait()
    def blur_own(h):
        lax.fori_loop(half_y, half_y + ny, blur_z(h), 0)
        if h == 0:
            pass_on(1, h)
        lax.fori_loop(pad, ny - pad, blur_y(h), 0)

    blur_own(0)
    lax.fori_loop(pad // ygroup, (ny - pad) // ygroup, blur_x((0,)), 0)
    pass_on(1, 1)

    def side_start(inner, last):
        return jnp.where((core == 0) == inner, last, 0)

    def from_row(body, first):
        return lambda i, carry: body(first + i, carry)

    def blur_edge(h, inner):
        if inner:
            for c in range(h * chunks // 2, (h + 1) * chunks // 2):
                inner_copy(c).wait_recv()
        else:
            pass_on(2, h)
        lax.fori_loop(0, half_y, from_row(blur_z(h), side_start(inner, half_y + ny)), 0)
        lax.fori_loop(0, pad, from_row(blur_y(h), side_start(inner, ny - pad)), 0)

    def blur_x_edge(cs, inner):
        first = side_start(inner, (ny - pad) // ygroup)
        lax.fori_loop(0, pad // ygroup, from_row(blur_x(cs), first), 0)

    blur_edge(0, True)
    blur_x_edge((0,), True)
    blur_edge(0, False)
    blur_x_edge((0,), False)

    halo = jnp.zeros((half_y, nz, nx), F32)

    @pl.when(jnp.logical_not(has_left))
    def _():
        q_ext[pl.ds(0, half_y)] = halo

    @pl.when(jnp.logical_not(has_right))
    def _():
        q_ext[pl.ds(half_y + ny, half_y)] = halo

    cov = jnp.full((nz, LANES), cov_ref[0, me_v].astype(F32), F32)
    count = cov_ref[0, 0]
    for v in range(1, nv):
        count = count + cov_ref[0, v]
    count = jnp.full((ny, LANES), count.astype(F32), F32)

    for c in range(chunks):
        own_planes(c).wait()
    reg_rows = reg.reshape(chunks, nz * ny, LANES)

    def qh_copy(c, side):
        target = me_t - 1 if side == 0 else me_t + 1
        rows = pl.ds(half_y, half_y) if side == 0 else pl.ds(ny, half_y)
        into = pl.ds(half_y + ny, half_y) if side == 0 else pl.ds(0, half_y)
        return pltpu.make_async_remote_copy(
            src_ref=q_ext.at[rows, :, lanes(c)],
            dst_ref=q_ext.at[into, :, lanes(c)],
            send_sem=qh_send.at[c, side],
            recv_sem=qh_recv.at[c, side],
            device_id=at(me_v, lax.rem(target + nt, nt)),
            device_id_type=MESH,
        )

    def quotient(c):
        arrived = reg.at[c, pl.ds(0, nz - planes)]
        pltpu.make_async_copy(arrived, arrived, a2a_recv.at[c]).wait()

        def body(y, carry):
            v = reg_rows[c, pl.ds(y, nz, stride=ny), :]
            q_ext[half_y + y, :, lanes(c)] = v / q_ext[half_y + y, :, lanes(c)]
            return carry

        lax.fori_loop(0, pad, from_row(body, side_start(False, ny - pad)), 0)

        @pl.when(jnp.logical_and(core == 0, has_left))
        def _():
            qh_copy(c, 0).start()

        @pl.when(jnp.logical_and(core == 1, has_right))
        def _():
            qh_copy(c, 1).start()

        lax.fori_loop(0, pad, from_row(body, side_start(True, ny - pad)), 0)

        @pl.when(core == 0)
        def _():
            qh_copy(c, 1).start()

        @pl.when(core == 1)
        def _():
            qh_copy(c, 0).start()

        lax.fori_loop(pad, ny - pad, body, 0)

    def back_rows(c, first, count):
        def body(i, carry):
            r = x_pass(wxt, zb, i * ygroup, ygroup, c, 0).reshape(ygroup, nz, LANES)
            for k in range(ygroup):
                reg_rows[c, pl.ds(i * ygroup + k, nz, stride=ny), :] = cov * r[k]
            return carry

        lax.fori_loop(0, count // ygroup, from_row(body, first // ygroup), 0)

    def back_pairs(c, first, count):
        def body(i, carry):
            for k in range(2):
                acc = py_ref[0, ky - 1] * q_ext[2 * i + k, :, lanes(c)]
                for b in range(1, ky):
                    acc = acc + py_ref[0, ky - 1 - b] * q_ext[2 * i + k + b, :, lanes(c)]
                yq[:, k * LANES : (k + 1) * LANES] = acc
            r = z_pass(azt, yq[...])
            for k in range(2):
                zb[2 * i + k, :, lanes(c)] = r[:, k * LANES : (k + 1) * LANES]
            return carry

        lax.fori_loop(0, count // 2, from_row(body, first // 2), 0)

    def back_inner(c):
        back_pairs(c, pad, ny - 2 * pad)

        @pl.when(core == 0)
        def _():
            qh_copy(c, 0).wait_recv()

        @pl.when(core == 1)
        def _():
            qh_copy(c, 1).wait_recv()

        first = side_start(True, ny - pad)
        back_pairs(c, first, pad)
        back_rows(c, pad, ny - 2 * pad)
        back_rows(c, first, pad)

    def back_outer(c):
        @pl.when(jnp.logical_and(core == 0, has_left))
        def _():
            qh_copy(c, 1).wait_recv()

        @pl.when(jnp.logical_and(core == 1, has_right))
        def _():
            qh_copy(c, 0).wait_recv()

        first = side_start(False, ny - pad)
        back_pairs(c, first, pad)
        back_rows(c, first, pad)

    sums = reg
    strip_rows = strip.reshape(strip_planes * ny, LANES)
    row = lax.broadcasted_iota(jnp.int32, (nz, LANES), 0)
    col = lax.broadcasted_iota(jnp.int32, (nz, LANES), 1)
    in_strip = lax.rem(row, packed) == col // STRIP

    def back_strip():
        def body(i, carry):
            r = x_pass(wm, zb, i * ygroup, ygroup, chunks, 0).reshape(ygroup, nz, LANES)
            for k in range(ygroup):
                v = jnp.where(in_strip, cov * r[k], 0.0)
                v = jnp.sum(v.reshape(strip_planes, packed, LANES), axis=1)
                strip_rows[pl.ds(i * ygroup + k, strip_planes, stride=ny), :] = v
            return carry

        lax.fori_loop(0, ny // ygroup, body, 0)

    def copy_to(src, dst, send, recv, c, u, d):
        return pltpu.make_async_remote_copy(
            src_ref=src,
            dst_ref=dst,
            send_sem=send.at[c, u, d],
            recv_sem=recv.at[c, u, d],
            device_id=at(up if d == 0 else down, me_t),
            device_id_type=MESH,
        )

    def shares(c):
        return range(1) if c == chunks else range(units)

    def s1_copy(c, u, d):
        if c == chunks:
            src, dst = strip.at[pl.ds(across * strip_blk + d * (strip_blk // 2), strip_blk // 2)], r1s.at[d]
        else:
            start = across * blk + u * sub + (0 if d == 0 else half)
            src, dst = sums.at[c, pl.ds(start, half)], r1.at[d, c, u]
        return copy_to(src, dst, s1_send, s1_recv, c, u, d)

    def s2_copy(c, u, d):
        owner = up if d == 0 else down
        if c == chunks:
            src, dst = strip.at[pl.ds(owner * strip_blk, strip_blk)], r2s.at[d]
        else:
            src, dst = sums.at[c, pl.ds(owner * blk + u * sub, sub)], r2.at[d, c, u]
        return copy_to(src, dst, s2_send, s2_recv, c, u, d)

    def g1_copy(c, u, d):
        if c == chunks:
            mine = strip_out.at[pl.ds(me_v * strip_blk, strip_blk)]
        else:
            mine = out_buf.at[pl.ds(me_v * blk + u * sub, sub), :, lanes(c)]
        return copy_to(mine, mine, g1_send, g1_recv, c, u, d)

    def g2_copy(c, u, d):
        owner = down if d == 0 else up
        if c == chunks:
            piece = strip_out.at[pl.ds(owner * strip_blk + d * (strip_blk // 2), strip_blk // 2)]
        else:
            start = owner * blk + u * sub + (0 if d == 0 else half)
            piece = out_buf.at[pl.ds(start, half), :, lanes(c)]
        return copy_to(piece, piece, g2_send, g2_recv, c, u, d)

    def stage1(c):
        for u in shares(c):
            for d in range(2):
                s1_copy(c, u, d).start()

    def stage2(c):
        for u in shares(c):
            for d in range(2):
                s1_copy(c, u, d).wait_recv()
                owner = up if d == 0 else down
                if c == chunks:
                    at_plane = pl.ds(owner * strip_blk + d * (strip_blk // 2), strip_blk // 2)
                    strip[at_plane] = strip[at_plane] + r1s[d]
                else:
                    start = owner * blk + u * sub + (0 if d == 0 else half)

                    def body(i, carry, u=u, d=d, start=start):
                        sums[c, start + i] = sums[c, start + i] + r1[d, c, u, i]
                        return carry

                    lax.fori_loop(0, half, body, 0)
                s2_copy(c, u, d).start()

    lane_row = lax.broadcasted_iota(jnp.int32, (ny, LANES), 1)
    own_rows = pl.ds(pad, ny)

    def stage3(c):
        for u in shares(c):
            for d in range(2):
                s2_copy(c, u, d).wait_recv()
            if c == chunks:

                def body(i, carry):
                    z = me_v * strip_blk + i
                    est = jnp.zeros((ny, LANES), F32)
                    for k in range(packed):
                        v = est_ext[chunks - 1, z * packed + k, own_rows, :]
                        v = pltpu.roll(v, (k * STRIP + half_x) % LANES, 1)
                        est = jnp.where(lane_row // STRIP == k, v, est)
                    merged = strip[z] + (r2s[0, i] + r2s[1, i])
                    strip_out[z] = est * merged / count
                    return carry

                lax.fori_loop(0, strip_blk, body, 0)
            else:

                def body(i, carry, u=u):
                    z = me_v * blk + u * sub + i
                    merged = sums[c, z] + (r2[0, c, u, i] + r2[1, c, u, i])
                    est = pltpu.roll(est_ext[c, z, own_rows, :], half_x, 1)
                    if c > 0:
                        before = pltpu.roll(est_ext[c - 1, z, own_rows, :], half_x, 1)
                        est = jnp.where(lane_row < half_x, before, est)
                    out_buf[z, :, lanes(c)] = est * merged / count
                    return carry

                lax.fori_loop(0, sub, body, 0)
            for d in range(2):
                g1_copy(c, u, d).start()

    def stage4(c):
        for u in shares(c):
            for d in range(2):
                g1_copy(c, u, d).wait_recv()
                g2_copy(c, u, d).start()

    def stage5(c):
        for u in shares(c):
            for d in range(2):
                g2_copy(c, u, d).wait_recv()

    def realign(c):
        for u in shares(c):
            for d in range(2):
                g1_copy(c, u, d).wait_send()
                g2_copy(c, u, d).wait_send()
        here = lane_row < LANES - half_x

        def body(i, carry):
            for k in range(packed):
                z = i * packed + k
                v = pltpu.roll(out_buf[z, :, lanes(c)], LANES - half_x, 1)
                if c == chunks - 1:
                    after = pltpu.roll(strip_out[i], (LANES - half_x - k * STRIP) % LANES, 1)
                else:
                    after = pltpu.roll(out_buf[z, :, lanes(c + 1)], LANES - half_x, 1)
                out_buf[z, :, lanes(c)] = jnp.where(here, v, after)
            return carry

        lax.fori_loop(0, nz // packed, body, 0)

    quotient(0)
    send_shared(1)
    back_inner(0)
    blur_own(1)
    blur_edge(1, True)
    back_outer(0)
    stage1(0)
    blur_edge(1, False)
    lax.fori_loop(0, ny // ygroup, blur_x((1,)), 0)
    stage2(0)
    quotient(1)
    send_shared(2)
    send_free(2)
    back_inner(1)
    stage3(0)
    back_outer(1)
    stage1(1)
    lax.fori_loop(0, ny // ygroup, blur_x((2, 3)), 0)
    stage4(0)
    stage2(1)
    quotient(2)
    send_shared(3)
    send_free(3)
    back_inner(2)
    stage3(1)
    back_outer(2)
    stage1(2)
    stage5(0)
    stage4(1)
    quotient(3)
    stage2(2)
    back_inner(3)
    back_outer(3)
    stage1(3)
    stage3(2)
    back_strip()
    stage1(chunks)
    stage5(1)
    realign(0)
    stage2(3)
    stage2(chunks)
    stage4(2)
    stage3(3)
    stage3(chunks)
    stage5(2)
    realign(1)
    stage4(3)
    stage4(chunks)
    stage5(3)
    realign(2)
    stage5(chunks)
    realign(3)

    for c in range(chunks):
        sent = reg.at[c, pl.ds(0, nz - planes)]
        pltpu.make_async_copy(sent, sent, a2a_send.at[c]).wait()

        inner_copy(c).wait_send()
    for c in range(chunks + 1):
        for u in shares(c):
            for d in range(2):
                s1_copy(c, u, d).wait_send()
                s2_copy(c, u, d).wait_send()
    for d in range(2):
        g1_copy(chunks, 0, d).wait_send()
        g2_copy(chunks, 0, d).wait_send()

    @pl.when(has_outer)
    def _():
        for c in range(chunks):
            outer_copy(c).wait_send()
        for n in range(2):
            for h in range(2):
                for d in range(2):
                    pass_copy(n, h, d).wait_send()

    @pl.when(has_left)
    def _():
        for c in range(chunks):
            qh_copy(c, 0).wait_send()

    @pl.when(has_right)
    def _():
        for c in range(chunks):
            qh_copy(c, 1).wait_send()


def solution(mesh):
    nv, nt = mesh.shape["view"], mesh.shape["tile"]

    def on_device(estimate, view_stacks, profile_z, profile_y, profile_x, offsets, coverage):
        nz, ny, nx = estimate.shape
        kz, ky, kx = profile_z.shape[1], profile_y.shape[1], profile_x.shape[1]
        planes = view_stacks.shape[1]
        tx = 4 if nt == 32 else 2
        chunks = nx // LANES
        pad = 8
        half_y = ky // 2
        blk = nz // nv
        sub = blk // UNITS
        strip_planes = nz * STRIP // LANES
        dims = (nv, nt, tx, nz, ny, nx, kz, ky, kx)
        any_spec = pl.BlockSpec(memory_space=pl.ANY)
        smem_spec = pl.BlockSpec(memory_space=pltpu.SMEM)
        dma = pltpu.SemaphoreType.DMA
        return pl.pallas_call(
            functools.partial(rl_kernel, dims),
            out_shape=pltpu.VMEM(estimate.shape, F32),
            in_specs=[any_spec, any_spec] + [smem_spec] * 5,
            out_specs=pl.BlockSpec(memory_space=pltpu.VMEM),
            scratch_shapes=[
                pltpu.VMEM(view_stacks.shape[1:], F32),
                pltpu.VMEM((chunks, nz, ny, LANES), F32),
                pltpu.VMEM((chunks, nz, ny + 2 * pad, LANES), F32),
                pltpu.VMEM((ny + 2 * half_y, nz, nx), F32),
                pltpu.VMEM((ny + 2 * half_y, nz, nx), F32),
                pltpu.VMEM((ny, nz, nx), F32),
                pltpu.VMEM((2, chunks, UNITS, sub // 2, ny, LANES), F32),
                pltpu.VMEM((2, chunks, UNITS, sub, ny, LANES), F32),
                pltpu.VMEM((nz, 2 * LANES), F32),
                pltpu.VMEM((2 * nz, 2 * nz), BF16),
                pltpu.VMEM((2 * nz, 2 * nz), BF16),
                pltpu.VMEM((3 * LANES, 2 * LANES), BF16),
                pltpu.VMEM((2 * LANES, 2 * LANES), BF16),
                pltpu.VMEM((LANES, 2 * LANES), BF16),
                pltpu.VMEM((strip_planes, ny, LANES), F32),
                pltpu.VMEM((strip_planes, ny, LANES), F32),
                pltpu.VMEM((2, strip_planes // nv // 2, ny, LANES), F32),
                pltpu.VMEM((2, strip_planes // nv, ny, LANES), F32),
                dma((planes,)),
                dma((chunks,)),
                dma((chunks,)),
                dma((chunks,)),
                dma((chunks,)),
                dma((chunks,)),
                dma((chunks,)),
                dma((2, 2, 2)),
                dma((2, 2, 2)),
                dma((chunks,)),
                dma((chunks,)),
            ]
            + [dma((chunks, 2))] * 2
            + [dma((chunks + 1, UNITS, 2))] * 8,
            compiler_params=pltpu.CompilerParams(
                collective_id=0, has_side_effects=True, vmem_limit_bytes=60_000_000
            ),
        )(estimate, view_stacks, profile_z, profile_y, profile_x, offsets, coverage)

    return jax.shard_map(
        on_device,
        mesh=mesh,
        in_specs=(
            P(None, "tile", None),
            P("view", "tile", None, None),
            P("view", None),
            P("view", None),
            P("view", None),
            P("view"),
            P("tile", None),
        ),
        out_specs=P(None, "tile", None),
        check_vma=False,
    )
```
